32 devices in a mesh: grp: 2 (over y), samp: 4 (over z), snp: 4 (over x, core).
Axes of the slice: x: 2, y: 2, z: 4, core: 2. Of those that a mesh axis runs over, the one named last changes fastest.
Arguments:
- genotypes: int32 [2048, 8192], P(('grp', 'samp'), 'snp'), parts along dimension 0, may hold values from 0 to 2730, as said below
- basis_cols: bfloat16 [16384, 256], P(('grp', 'snp')), parts along dimension 0, may hold values from -0.0625 to 0.0625
Outputs:
- y_block: float32 [8, 4, 512, 256], P(('grp', 'snp'), 'samp'), parts along dimension 0
- r_factor: float32 [512, 256], P('grp'), parts along dimension 0
- q_next: float32 [8, 4, 512, 256], P(('grp', 'snp'), 'samp'), parts along dimension 0
The draws below stay inside these ranges and needn't reach their ends.
There are 2 independent parts, one for each index of `grp`. The reference program is written for one: setup_inputs(seed, part) draws one part's arguments, and reference() takes and returns one part's arrays. A program takes and returns all parts, laid end to end along the dimension named above; each array names one. Nothing has to cross between parts.
Inputs may be any that keep to these rules, and one draw needn't show every extreme that they name: `genotypes`: each word packs 6 dosages of 0, 1 or 2 in pairs of bits: bits 2 t and 2 t + 1 of word (w, p) hold the dosage of sample 6 w + t at SNP p, t from 0 to 5; bits 12 and up are zero.
All inputs are finite; a program needn't handle non-finite values.
Results may differ from the reference program's by a relative error of at most 0.0025.
Values may be sent and summed in bfloat16 or wider, within the bound.
A program may use at most 64 MiB of HBM per device.

```python
import math
import jax
import jax.numpy as jnp
from jax import lax

K = 256
PD = 2048
WD = 256
NP = 8192
N_SAMP = 4
N_SNP = 4


def draw_genotypes(key, part):
    key_base = jax.random.fold_in(key, 11)
    key_drift = jax.random.fold_in(key, 12)
    key_dose = jax.random.fold_in(key, 13)
    word_count = WD * N_SAMP
    snp_count = PD * N_SNP
    base_freq = jax.random.randint(key_base, (snp_count,), 10, 91)
    drift_level = jax.random.randint(key_drift, (N_SAMP, snp_count), 0, 3)
    frequency = base_freq[None, :] * (1 + drift_level) // 3
    freq_rows = jnp.repeat(frequency, WD, axis=0)
    packed = jnp.zeros((word_count, snp_count), jnp.int32)
    for plane_idx in range(6):
        plane_key = jax.random.fold_in(key_dose, plane_idx)
        first_draw = jax.random.randint(jax.random.fold_in(plane_key, 1), (word_count, snp_count), 0, 100)
        second_draw = jax.random.randint(jax.random.fold_in(plane_key, 2), (word_count, snp_count), 0, 100)
        dose_plane = (first_draw < freq_rows).astype(jnp.int32) + (second_draw < freq_rows).astype(jnp.int32)
        packed = packed + dose_plane * 4 ** plane_idx
    return packed


def levels(own_key, dims, pieces, least, top_value):
    level = 1.0
    for dim, parts in pieces:
        heights = jax.random.uniform(jax.random.fold_in(jax.random.fold_in(own_key, 6), dim), (parts,), jnp.float32, least / len(pieces), top_value / len(pieces))
        level = level * jnp.repeat(jnp.exp(heights), dims[dim] // parts).reshape((-1,) + (1,) * (len(dims) - 1 - dim))
    return level


def scatter_about(own_key, dims, deviation, reach, cuts=(), held_as=jnp.bfloat16):
    loudness = levels(own_key, dims, cuts, -0.22, 0.18) if cuts else 1.0
    drawn = jax.random.normal(own_key, dims, jnp.float32) * deviation * loudness
    return jnp.minimum(jnp.maximum(drawn, -reach), reach).astype(held_as)


def setup_inputs(seed: int = 0, part: int = 0) -> dict:
    arg_keys = jax.random.split(jax.random.key(seed), 3)
    part_keys = jax.random.split(jax.random.fold_in(arg_keys[2], part), 3)
    genotypes = draw_genotypes(jax.random.fold_in(jax.random.fold_in(arg_keys[2], part), 71), part)
    basis_cols = scatter_about(part_keys[1], (NP, K), NP ** -0.5, 0.0625, ((0, 4),))
    return {"genotypes": genotypes, "basis_cols": basis_cols}


def unpack(word_block):
    planes = [jnp.bitwise_and(jnp.right_shift(word_block, 2 * shift_pos), 3) for shift_pos in range(6)]
    return jnp.stack(planes, axis=1).reshape(word_block.shape[0] * 6, word_block.shape[1])

def reference(genotypes, basis_cols):
    word_count, snp_count = genotypes.shape
    samples = word_count * 6
    block_words = math.gcd(word_count, 64)
    blocks = genotypes.reshape(word_count // block_words, block_words, snp_count)

    def count_block(running, word_block):
        return (running + lax.optimization_barrier(jnp.sum(unpack(word_block), axis=0)).astype(jnp.int32), None)
    counts, unused = lax.scan(count_block, jnp.zeros((snp_count,), jnp.int32), blocks)
    allele_mean = counts.astype(jnp.float32) / jnp.float32(samples)
    center = jnp.dot(allele_mean, basis_cols.astype(jnp.float32), precision=lax.Precision.HIGHEST)

    def project_block(running, word_block):
        dosage = unpack(word_block).astype(jnp.bfloat16)
        scores = (jnp.dot(dosage.astype(jnp.float32), basis_cols.astype(jnp.float32), preferred_element_type=jnp.float32) - center[None, :]).astype(jnp.bfloat16)
        return (running + lax.dot_general(dosage.astype(jnp.float32), scores.astype(jnp.float32), (((0,), (0,)), ((), ())), preferred_element_type=jnp.float32), None)
    y_full, unused = lax.scan(project_block, jnp.zeros((snp_count, basis_cols.shape[1]), jnp.float32), blocks)
    y_full = y_full * (jnp.float32(1.0) / jnp.sqrt(jnp.float32(samples)))
    gram_sum = jnp.dot(y_full.T, y_full, precision=lax.Precision.HIGHEST) / jnp.float32(snp_count)
    lower_factor = jnp.linalg.cholesky(gram_sum)
    q_next = lax.linalg.triangular_solve(lower_factor, y_full, left_side=False, lower=True, transpose_a=True)
    layout = (N_SNP, N_SAMP, snp_count // (N_SNP * N_SAMP), basis_cols.shape[1])
    return (y_full.reshape(layout), lower_factor.T, q_next.reshape(layout))
```

```python
import functools
import jax
import jax.numpy as jnp
from jax import lax
from jax.experimental import pallas as pl
from jax.experimental.pallas import tpu as pltpu
from jax.sharding import PartitionSpec as P

PLANES = 6
MESH = pl.DeviceIdType.MESH
F32 = jnp.float32
BF16 = jnp.bfloat16
HIGH = lax.Precision.HIGHEST
LEVELS = 32767.0


def log2(n):
    bits = n.bit_length() - 1
    assert 1 << bits == n
    return bits


def each(count, body):
    if count <= 16:
        for i in range(count):
            body(i)
    else:
        lax.fori_loop(0, count, lambda i, carry: (body(i), carry)[1], 0)


def pieces(rows, devices):
    size = max(8, rows // devices)
    return size, rows // size


def main_kernel(
    n_snp, n_samp,
    g_hbm, b_hbm, y_ref, gram_ref,
    g_ref, b_ref, part, rs_rx, coded, coded_rx, meta, meta_rx, scores, dose_t,
    cs_tx, cs_rx, ct_tx, ct_rx, y_own, y_tmp, yq, ysc, yq_rx, ysc_rx,
    ga_w, ga_rx, ga_out, gb_w, gb_rx, gb_out,
    in_s, rs_s, rs_r, ex_s, ex_r, mt_s, mt_r, ag_s, ag_r, cs_s, cs_r, ct_s, ct_r,
    yq_s, yq_r, ysc_s, ysc_r, ga_s, ga_r, ha_s, ha_r, gb_s, gb_r, hb_s, hb_r,
):
    snp, samp = lax.axis_index("snp"), lax.axis_index("samp")
    bits = log2(n_snp)
    devices = n_snp * n_samp
    me = samp * n_snp + snp
    words = g_ref.shape[0]
    rows = PLANES * words
    halves, _, lanes = scores.shape
    width = halves * lanes
    chunks = coded.shape[2]
    cwords = words // chunks
    crow = PLANES * cwords
    krow = crow // 2
    per = PLANES // 2
    samples = rows * n_samp
    own_rows = y_own.shape[1]
    bit = lax.rem(snp, 2)

    def copy(src, dst, ssem, rsem, **peer):
        return pltpu.make_async_remote_copy(
            src_ref=src, dst_ref=dst, send_sem=ssem, recv_sem=rsem,
            device_id=peer, device_id_type=MESH,
        )

    def partner(b):
        return snp + (1 << b) * (1 - 2 * ((snp // (1 << b)) % 2))

    def load_b():
        return pltpu.make_async_copy(b_hbm, b_ref, in_s.at[chunks])

    def load_g(c):
        seg = pl.ds(c * cwords, cwords)
        return pltpu.make_async_copy(g_hbm.at[seg], g_ref.at[seg], in_s.at[c])

    load_g(0).start()
    load_b().start()
    for c in range(1, chunks):
        load_g(c).start()
    barrier = pltpu.get_barrier_semaphore()

    def greet(i):
        peer = lax.rem(me + 1 + i, devices)
        pl.semaphore_signal(
            barrier, inc=1, device_id={"samp": peer // n_snp, "snp": lax.rem(peer, n_snp)}, device_id_type=MESH
        )

    each(devices - 1, greet)

    def at(c, side, size):
        return pl.ds(pl.multiple_of(c * crow + side * krow, 16), size)

    def rs_copy(c):
        return copy(part.at[at(c, 1 - bit, krow)], rs_rx.at[pl.ds(c * krow, krow)],
                    rs_s.at[c], rs_r.at[c], snp=partner(0))

    colsum = jnp.zeros((8, width), F32)

    def product(c, side):
        total = jnp.zeros((8, width), F32)
        for i in range(per):
            t = side * per + i
            word = g_ref[c * cwords:(c + 1) * cwords, :]
            dose = (lax.shift_right_logical(word, jnp.full_like(word, 2 * t)) & 3).astype(F32).astype(BF16)
            prod = jnp.dot(dose, b_ref[...], preferred_element_type=F32)
            part[pl.ds(pl.multiple_of(c * crow + t * cwords, 16), cwords), :] = prod
            total = total + prod.reshape(cwords // 8, 8, width).sum(axis=0)
        return total

    load_b().wait()
    for c in range(chunks):
        load_g(c).wait()
        colsum = colsum + product(c, 1 - bit)
        if c == 0:
            pl.semaphore_wait(barrier, devices - 1)
        rs_copy(c).start()
    for c in range(chunks):
        colsum = colsum + product(c, bit)
    cs_tx[...] = colsum

    def cs_copy(d):
        return copy(cs_tx, cs_rx.at[d], cs_s.at[d], cs_r.at[d], snp=lax.rem(snp + d, n_snp))

    def ct_copy(d):
        return copy(ct_tx, ct_rx.at[d], ct_s.at[d], ct_r.at[d], samp=lax.rem(samp + d, n_samp))

    each(n_snp - 1, lambda i: cs_copy(i + 1).start())

    def ex_copies(b, h, c):
        return (
            copy(coded.at[b - 1, h, c], coded_rx.at[b - 1, h, c], ex_s.at[b - 1, h, c], ex_r.at[b - 1, h, c], snp=partner(b)),
            copy(meta.at[b - 1, h, c], meta_rx.at[b - 1, h, c], mt_s.at[b - 1, h, c], mt_r.at[b - 1, h, c], snp=partner(b)),
        )

    def code(b, h, c):
        block = part[at(c, bit, krow), h * lanes:(h + 1) * lanes]
        mean = jnp.sum(block, axis=0, keepdims=True) * F32(1.0 / krow)
        block = block - mean
        top = jnp.maximum(jnp.max(jnp.abs(block), axis=0, keepdims=True), F32(1e-30))
        coded[b - 1, h, c] = jnp.round(block * (F32(LEVELS) / top)).astype(jnp.int32).astype(jnp.int16)
        first = lax.broadcasted_iota(jnp.int32, (8, lanes), 0) == 0
        meta[b - 1, h, c] = jnp.where(first, top * F32(1.0 / LEVELS), mean)
        for cp in ex_copies(b, h, c):
            cp.start()

    def arrived(b, h, c):
        for cp in ex_copies(b, h, c):
            cp.wait()
        other = coded_rx[b - 1, h, c].astype(jnp.int32).astype(F32) * meta_rx[b - 1, h, c, 0:1, :]
        return part[at(c, bit, krow), h * lanes:(h + 1) * lanes] + (other + meta_rx[b - 1, h, c, 1:2, :])

    def ag_copy(h, c):
        seg = at(c, bit, krow)
        return copy(scores.at[h, seg], scores.at[h, seg], ag_s.at[h, c], ag_r.at[h, c], snp=partner(0))

    for c in range(chunks):
        rs_copy(c).wait()
        seg = at(c, bit, krow)
        part[seg, :] = part[seg, :] + rs_rx[c * krow:(c + 1) * krow, :]
        if bits > 1:
            code(1, 0, c)
    if bits > 1:
        for h in range(1, halves):
            for c in range(chunks):
                code(1, h, c)

    each(n_snp - 1, lambda i: cs_copy(i + 1).wait())
    tot = colsum
    for d in range(1, n_snp):
        tot = tot + cs_rx[d]
    ct_tx[...] = tot
    each(n_samp - 1, lambda i: ct_copy(i + 1).start())
    word_t = g_ref[...].T
    for c in range(chunks):
        for t in range(PLANES):
            off = c * crow + t * cwords
            dose_t[:, off:off + cwords] = ((word_t[:, c * cwords:(c + 1) * cwords] >> (2 * t)) & 3).astype(F32).astype(BF16)
    for b in range(2, bits):
        for h in range(halves):
            for c in range(chunks):
                part[at(c, bit, krow), h * lanes:(h + 1) * lanes] = arrived(b - 1, h, c)
                code(b, h, c)
    each(n_samp - 1, lambda i: ct_copy(i + 1).wait())
    for d in range(1, n_samp):
        tot = tot + ct_rx[d]
    center = tot.sum(axis=0, keepdims=True) / F32(samples)

    def finish_scores(h):
        for c in range(chunks):
            seg = at(c, bit, krow)
            if bits > 1:
                total = arrived(bits - 1, h, c)
            else:
                total = part[seg, h * lanes:(h + 1) * lanes]
            scores[h, seg, :] = (total - center[:, h * lanes:(h + 1) * lanes]).astype(BF16)
            ag_copy(h, c).start()

    def gather_scores(h):
        for c in range(chunks):
            ag_copy(h, c).wait()

    inv_root = F32(1.0) / jnp.sqrt(F32(samples))
    last = n_samp - 1
    relay = n_samp >= 4
    mirrored = samp >= n_samp // 2
    place = jnp.where(mirrored, last - samp, samp)
    slots = n_samp - 1

    def y_part(h, owner):
        blk = dose_t[pl.ds(pl.multiple_of(owner * own_rows, 16), own_rows), :]
        return jnp.dot(blk, scores[h], preferred_element_type=F32) * inv_root

    def owner_of(k):
        v = lax.rem(place + jnp.where(place == 0, last - k, jnp.where(k == 0, last, k)), n_samp)
        return jnp.where(mirrored, last - v, v)

    def y_copies(h, k):
        to, slot = owner_of(k), samp
        if relay:
            handed = jnp.logical_and(place == 0, k == 0)
            to = jnp.where(handed, jnp.where(mirrored, last - 1, 1), to)
            slot = jnp.where(handed, to, samp)
        return (
            copy(yq.at[h, k], yq_rx.at[h, slot], yq_s.at[h, k], yq_r.at[h, slot], samp=to),
            copy(ysc.at[h, k], ysc_rx.at[h, slot], ysc_s.at[h, k], ysc_r.at[h, slot], samp=to),
        )

    def y_wait(h, slot):
        copy(yq.at[h, 0], yq_rx.at[h, slot], yq_s.at[h, 0], yq_r.at[h, slot], samp=samp).wait_recv()
        copy(ysc.at[h, 0], ysc_rx.at[h, slot], ysc_s.at[h, 0], ysc_r.at[h, slot], samp=samp).wait_recv()

    def y_decode(h, slot):
        return yq_rx[h, slot].astype(jnp.int32).astype(F32) * ysc_rx[h, slot, 0:1, :]

    def y_send(h, k, block):
        top = jnp.maximum(jnp.max(jnp.abs(block), axis=0, keepdims=True), F32(1e-30))
        yq[h, k] = jnp.round(block * (F32(LEVELS) / top)).astype(jnp.int32).astype(jnp.int16)
        ysc[h, k] = jnp.broadcast_to(top * F32(1.0 / LEVELS), (8, lanes))
        for cp in y_copies(h, k):
            cp.start()

    def y_early(h):
        each(slots - 1 if relay else slots, lambda k: y_send(h, k, y_part(h, owner_of(k))))
        if relay:
            @pl.when(place != 1)
            def _():
                y_send(h, slots - 1, y_part(h, owner_of(slots - 1)))

            @pl.when(place == 1)
            def _():
                y_tmp[h] = y_part(h, owner_of(slots - 1))
        y_own[h] = y_part(h, samp)

    def y_merge(h):
        if relay:
            @pl.when(place == 1)
            def _():
                y_wait(h, samp)
                y_send(h, slots - 1, y_tmp[h] + y_decode(h, samp))

    def y_finish(h):
        def add(i):
            src = lax.rem(samp + 1 + i, n_samp)
            if relay:
                @pl.when(jnp.logical_or(place != 0, src != last - samp))
                def _():
                    y_wait(h, src)
                    y_own[h] = y_own[h] + y_decode(h, src)
            else:
                y_wait(h, src)
                y_own[h] = y_own[h] + y_decode(h, src)

        each(slots, add)
        y_ref[:, h * lanes:(h + 1) * lanes] = y_own[h]

    snp_total = F32(dose_t.shape[0] * n_snp)

    def gram_of(a, b):
        return lax.dot_general(a, b, (((0,), (0,)), ((), ())), precision=HIGH, preferred_element_type=F32) / snp_total

    def all_sum(work, rx, out, s1, r1, s2, r2):
        size, owners = pieces(work.shape[0], devices)

        def peer_of(i):
            return lax.rem(me + 1 + i, devices)

        def piece(i):
            return pl.ds(pl.multiple_of(i * size, 8), size)

        def where_owner(i, body):
            if owners == devices:
                body()
            else:
                pl.when(i < owners)(body)

        def one(i):
            p = peer_of(i)
            return p, copy(work.at[piece(p)], rx.at[me], s1.at[p], r1.at[me], samp=p // n_snp, snp=lax.rem(p, n_snp))

        def two(i):
            p = peer_of(i)
            return p, copy(out.at[piece(me)], out.at[piece(me)], s2.at[p], r2.at[me], samp=p // n_snp, snp=lax.rem(p, n_snp))

        def start():
            def go(i):
                p, cp = one(i)
                where_owner(p, lambda: cp.start())
            each(devices - 1, go)

        def middle():
            def owned():
                rx[me] = work[piece(me), :]

                def got(i):
                    p = peer_of(i)
                    copy(work.at[piece(0)], rx.at[p], s1.at[p], r1.at[p], samp=samp).wait_recv()
                each(devices - 1, got)
                total = lax.fori_loop(1, devices, lambda j, acc: acc + rx[j], rx[0], unroll=devices <= 16)
                out[piece(me), :] = total
                each(devices - 1, lambda i: two(i)[1].start())
            where_owner(me, owned)

        def finish():
            def got(i):
                p = peer_of(i)
                where_owner(p, lambda: copy(out.at[piece(0)], out.at[piece(p)], s2.at[p], r2.at[p], samp=samp).wait_recv())
            each(devices - 1, got)

        def drain():
            def sent(i):
                p, cp = one(i)
                where_owner(p, lambda: cp.wait_send())
            each(devices - 1, sent)
            where_owner(me, lambda: each(devices - 1, lambda i: two(i)[1].wait_send()))

        return start, middle, finish, drain

    a_start, a_middle, a_finish, a_drain = all_sum(ga_w, ga_rx, ga_out, ga_s, ga_r, ha_s, ha_r)
    b_start, b_middle, b_finish, b_drain = all_sum(gb_w, gb_rx, gb_out, gb_s, gb_r, hb_s, hb_r)

    finish_scores(0)
    gather_scores(0)
    y_early(0)
    finish_scores(1)
    gather_scores(1)
    y_early(1)
    y_merge(0)
    y_merge(1)
    y_finish(0)
    ga_w[...] = gram_of(y_own[0], y_own[0])
    a_start()
    a_middle()
    y_finish(1)
    gb_w[:lanes, :] = gram_of(y_own[0], y_own[1])
    gb_w[lanes:, :] = gram_of(y_own[1], y_own[1])
    b_start()
    a_finish()
    gram_ref[:lanes, :lanes] = ga_out[...]
    gram_ref[lanes:, :lanes] = jnp.zeros((lanes, lanes), F32)
    b_middle()
    b_finish()
    gram_ref[:, lanes:] = gb_out[...]
    for h in range(halves):
        def sent(k):
            for cp in y_copies(h, k):
                cp.wait_send()
        each(slots, sent)
    a_drain()
    b_drain()


def eliminate(a):
    n = a.shape[0]
    groups = n // 8
    lane = lax.broadcasted_iota(jnp.int32, (8, n), 1)
    sub = lax.broadcasted_iota(jnp.int32, (8, n), 0)
    left = [a[8 * g:8 * g + 8, :] for g in range(groups)]
    right = [jnp.where(lane == sub + 8 * g, F32(1.0), F32(0.0)) for g in range(groups)]

    def across(x, j):
        return jnp.broadcast_to(x[:, j:j + 1], (8, n))

    def down(x, s):
        return jnp.broadcast_to(x[s:s + 1, :], (8, n))

    for g0 in range(groups):
        jl, jr = left[g0], right[g0]
        cols = [across(jl, 8 * g0 + i) for i in range(8)]
        up_l, up_r = jl, jr
        for s in range(0, 8, 2):
            c0, c1 = cols[s], cols[s + 1]
            a00, a10, a11 = down(c0, s), down(c0, s + 1), down(c1, s + 1)
            inv_a = F32(1.0) / a00
            inv_det = F32(1.0) / (a00 * a11 - a10 * a10)
            m = a10 * inv_a
            f = a00 * inv_det

            def step(x):
                u, v = down(x, s), down(x, s + 1)
                v = v - m * u
                w1 = v * f
                w0 = u * inv_a - m * w1
                x = x - c0 * w0 - c1 * w1
                return u, v, jnp.where(sub == s, w0, jnp.where(sub == s + 1, w1, x))

            for i in range(s + 2, 8):
                cols[i] = step(cols[i])[2]
            u, v, jl = step(jl)
            up_l = jnp.where(sub == s, u, jnp.where(sub == s + 1, v, up_l))
            u, v, jr = step(jr)
            up_r = jnp.where(sub == s, u, jnp.where(sub == s + 1, v, up_r))
        left[g0], right[g0] = up_l, up_r
        rows_l = [down(jl, i) for i in range(8)]
        rows_r = [down(jr, i) for i in range(8)]
        for g in range(g0 + 1, groups):
            xl, xr = left[g], right[g]
            for i in range(8):
                col = across(left[g], 8 * g0 + i)
                xl = xl - col * rows_l[i]
                xr = xr - col * rows_r[i]
            left[g], right[g] = xl, xr
    ups, invs = [], []
    for g in range(groups):
        diag = jnp.sum(jnp.where(lane == sub + 8 * g, left[g], F32(0.0)), axis=1, keepdims=True)
        scale = F32(1.0) / jnp.sqrt(diag)
        ups.append(jnp.where(lane >= sub + 8 * g, left[g] * scale, F32(0.0)))
        invs.append(right[g] * scale)
    return jnp.concatenate(ups, axis=0), jnp.concatenate(invs, axis=0)


def factor_kernel(gram_in, y_ref, y_out, r_ref, q_ref, inv_ref, gram_ref, y_sem):
    y_copy = pltpu.make_async_copy(y_ref, y_out, y_sem)
    y_copy.start()
    width = gram_in.shape[0]
    on = lax.broadcasted_iota(jnp.int32, (width, width), 0) == lax.broadcasted_iota(jnp.int32, (width, width), 1)
    kept = jnp.where(on, gram_in[...], F32(0.0))
    d_row = jnp.sqrt(jnp.sum(kept, axis=0, keepdims=True))
    d_col = jnp.sqrt(jnp.sum(kept, axis=1, keepdims=True))
    gram_ref[...] = gram_in[...] * (F32(1.0) / d_col) * (F32(1.0) / d_row)
    nb = min(128, width)
    blocks = width // nb

    def blk(ref, i, j):
        return ref[i * nb:(i + 1) * nb, j * nb:(j + 1) * nb]

    def dot(a, b, dims):
        return lax.dot_general(a, b, (dims, ((), ())), precision=HIGH, preferred_element_type=F32)

    r_ref[...] = jnp.zeros_like(r_ref)
    inv_ref[...] = jnp.zeros_like(inv_ref)
    for k in range(blocks):
        a = blk(gram_ref, k, k)
        for m in range(k):
            a = a - dot(blk(r_ref, m, k), blk(r_ref, m, k), ((0,), (0,)))
        upper, inv = eliminate(a)
        r_ref[k * nb:(k + 1) * nb, k * nb:(k + 1) * nb] = upper
        inv_ref[k * nb:(k + 1) * nb, k * nb:(k + 1) * nb] = inv
        for j in range(k + 1, blocks):
            a = blk(gram_ref, k, j)
            for m in range(k):
                a = a - dot(blk(r_ref, m, k), blk(r_ref, m, j), ((0,), (0,)))
            r_ref[k * nb:(k + 1) * nb, j * nb:(j + 1) * nb] = dot(inv, a, ((1,), (0,)))
        for j in range(k):
            acc = jnp.zeros((nb, nb), F32)
            for m in range(j, k):
                acc = acc + dot(blk(r_ref, m, k), blk(inv_ref, m, j), ((0,), (0,)))
            inv_ref[k * nb:(k + 1) * nb, j * nb:(j + 1) * nb] = -dot(inv, acc, ((1,), (0,)))
    r_ref[...] = r_ref[...] * d_row
    q_ref[...] = dot(y_ref[...] * (F32(1.0) / d_row), inv_ref[...], ((1,), (1,)))
    y_copy.wait()


def per_device(n_snp, n_samp, genotypes, basis_cols):
    words, snps = genotypes.shape
    width = basis_cols.shape[1]
    rows = PLANES * words
    lanes = width // 2
    chunks = max(1, words // 128)
    own = snps // n_samp
    bits = log2(n_snp)
    devices = n_snp * n_samp
    krow = rows // chunks // 2
    steps = max(1, bits - 1)
    vmem = pl.BlockSpec(memory_space=pltpu.VMEM)
    hbm = pl.BlockSpec(memory_space=pl.ANY)
    dma = pltpu.SemaphoreType.DMA
    size_a, size_b = pieces(lanes, devices)[0], pieces(width, devices)[0]
    y, gram = pl.pallas_call(
        functools.partial(main_kernel, n_snp, n_samp),
        out_shape=(
            jax.ShapeDtypeStruct((own, width), F32),
            jax.ShapeDtypeStruct((width, width), F32),
        ),
        in_specs=[hbm, hbm],
        out_specs=(vmem, vmem),
        scratch_shapes=[
            pltpu.VMEM((words, snps), jnp.int32),
            pltpu.VMEM((snps, width), BF16),
            pltpu.VMEM((rows, width), F32),
            pltpu.VMEM((rows // 2, width), F32),
            pltpu.VMEM((steps, 2, chunks, krow, lanes), jnp.int16),
            pltpu.VMEM((steps, 2, chunks, krow, lanes), jnp.int16),
            pltpu.VMEM((steps, 2, chunks, 8, lanes), F32),
            pltpu.VMEM((steps, 2, chunks, 8, lanes), F32),
            pltpu.VMEM((2, rows, lanes), BF16),
            pltpu.VMEM((snps, rows), BF16),
            pltpu.VMEM((8, width), F32),
            pltpu.VMEM((n_snp, 8, width), F32),
            pltpu.VMEM((8, width), F32),
            pltpu.VMEM((n_samp, 8, width), F32),
            pltpu.VMEM((2, own, lanes), F32),
            pltpu.VMEM((2, own, lanes), F32),
            pltpu.VMEM((2, n_samp, own, lanes), jnp.int16),
            pltpu.VMEM((2, n_samp, 8, lanes), F32),
            pltpu.VMEM((2, n_samp, own, lanes), jnp.int16),
            pltpu.VMEM((2, n_samp, 8, lanes), F32),
            pltpu.VMEM((lanes, lanes), F32),
            pltpu.VMEM((devices, size_a, lanes), F32),
            pltpu.VMEM((lanes, lanes), F32),
            pltpu.VMEM((width, lanes), F32),
            pltpu.VMEM((devices, size_b, lanes), F32),
            pltpu.VMEM((width, lanes), F32),
            dma((chunks + 1,)),
            dma((chunks,)), dma((chunks,)),
            dma((steps, 2, chunks)), dma((steps, 2, chunks)), dma((steps, 2, chunks)), dma((steps, 2, chunks)),
            dma((2, chunks)), dma((2, chunks)),
            dma((n_snp,)), dma((n_snp,)), dma((n_samp,)), dma((n_samp,)),
            dma((2, n_samp)), dma((2, n_samp)), dma((2, n_samp)), dma((2, n_samp)),
            dma((devices,)), dma((devices,)), dma((devices,)), dma((devices,)),
            dma((devices,)), dma((devices,)), dma((devices,)), dma((devices,)),
        ],
        compiler_params=pltpu.CompilerParams(
            collective_id=0, has_side_effects=True, vmem_limit_bytes=48 * 1024 * 1024
        ),
    )(genotypes, basis_cols)
    y, r_factor, q_next = pl.pallas_call(
        factor_kernel,
        out_shape=(
            jax.ShapeDtypeStruct((own, width), F32),
            jax.ShapeDtypeStruct((width, width), F32),
            jax.ShapeDtypeStruct((own, width), F32),
        ),
        in_specs=[vmem, vmem],
        out_specs=(pl.BlockSpec(memory_space=pl.ANY), vmem, vmem),
        scratch_shapes=[
            pltpu.VMEM((width, width), F32),
            pltpu.VMEM((width, width), F32),
            pltpu.SemaphoreType.DMA,
        ],
    )(gram, y)
    layout = (1, 1, own, width)
    return (y.reshape(layout), r_factor, q_next.reshape(layout))


def solution(mesh):
    return jax.shard_map(
        functools.partial(per_device, mesh.shape["snp"], mesh.shape["samp"]),
        mesh=mesh,
        in_specs=(P(("grp", "samp"), "snp"), P(("grp", "snp"), None)),
        out_specs=(
            P(("grp", "snp"), "samp", None, None),
            P("grp", None),
            P(("grp", "snp"), "samp", None, None),
        ),
        check_vma=False,
    )
```

```python
import functools
import jax
import jax.numpy as jnp
from jax import lax
from jax.experimental import pallas as pl
from jax.experimental.pallas import tpu as pltpu
from jax.sharding import PartitionSpec as P

PLANES = 6
MESH = pl.DeviceIdType.MESH
F32 = jnp.float32
BF16 = jnp.bfloat16
HIGH = lax.Precision.HIGHEST
LEVELS = 32767.0


def log2(n):
    bits = n.bit_length() - 1
    assert 1 << bits == n
    return bits


def eliminate(a, pause=None):
    n = a.shape[0]
    groups = n // 8
    lane = lax.broadcasted_iota(jnp.int32, (8, n), 1)
    sub = lax.broadcasted_iota(jnp.int32, (8, n), 0)
    left = [a[8 * g:8 * g + 8, :] for g in range(groups)]
    right = [jnp.where(lane == sub + 8 * g, F32(1.0), F32(0.0)) for g in range(groups)]

    def across(x, j):
        return jnp.broadcast_to(x[:, j:j + 1], (8, n))

    def down(x, s):
        return jnp.broadcast_to(x[s:s + 1, :], (8, n))

    for g0 in range(groups):
        if pause is not None and g0 == groups // 2:
            pause()
        jl, jr = left[g0], right[g0]
        cols = [across(jl, 8 * g0 + i) for i in range(8)]
        up_l, up_r = jl, jr
        for s in range(0, 8, 2):
            c0, c1 = cols[s], cols[s + 1]
            a00, a10, a11 = down(c0, s), down(c0, s + 1), down(c1, s + 1)
            inv_a = F32(1.0) / a00
            inv_det = F32(1.0) / (a00 * a11 - a10 * a10)
            m = a10 * inv_a
            f = a00 * inv_det

            def step(x):
                u, v = down(x, s), down(x, s + 1)
                v = v - m * u
                w1 = v * f
                w0 = u * inv_a - m * w1
                x = x - c0 * w0 - c1 * w1
                return u, v, jnp.where(sub == s, w0, jnp.where(sub == s + 1, w1, x))

            for i in range(s + 2, 8):
                cols[i] = step(cols[i])[2]
            u, v, jl = step(jl)
            up_l = jnp.where(sub == s, u, jnp.where(sub == s + 1, v, up_l))
            u, v, jr = step(jr)
            up_r = jnp.where(sub == s, u, jnp.where(sub == s + 1, v, up_r))
        left[g0], right[g0] = up_l, up_r
        rows_l = [down(jl, i) for i in range(8)]
        rows_r = [down(jr, i) for i in range(8)]
        for g in range(g0 + 1, groups):
            xl, xr = left[g], right[g]
            for i in range(8):
                col = across(left[g], 8 * g0 + i)
                xl = xl - col * rows_l[i]
                xr = xr - col * rows_r[i]
            left[g], right[g] = xl, xr
    ups, invs = [], []
    for g in range(groups):
        diag = jnp.sum(jnp.where(lane == sub + 8 * g, left[g], F32(0.0)), axis=1, keepdims=True)
        scale = F32(1.0) / jnp.sqrt(diag)
        ups.append(jnp.where(lane >= sub + 8 * g, left[g] * scale, F32(0.0)))
        invs.append(right[g] * scale)
    return jnp.concatenate(ups, axis=0), jnp.concatenate(invs, axis=0)


def dot(a, b, dims):
    return lax.dot_general(a, b, (dims, ((), ())), precision=HIGH, preferred_element_type=F32)


def diagonal(block):
    n = block.shape[0]
    on = lax.broadcasted_iota(jnp.int32, (n, n), 0) == lax.broadcasted_iota(jnp.int32, (n, n), 1)
    kept = jnp.where(on, block, F32(0.0))
    row = jnp.sqrt(jnp.sum(kept, axis=0, keepdims=True))
    col = jnp.sqrt(jnp.sum(kept, axis=1, keepdims=True))
    return row, col


def scaled(block, col, row):
    return block * (F32(1.0) / col) * (F32(1.0) / row)


def factor_kernel(gb_ref, up_ref, inv_ref, d_ref, y_ref, y_out, r_out, q_out, r_ref, q_ref, sems):
    lanes = up_ref.shape[0]
    y_copy = pltpu.make_async_copy(y_ref, y_out, sems.at[0])
    y_copy.start()
    d0_row = d_ref[0:1, :]
    d0_col = jnp.broadcast_to(d0_row, (lanes, lanes)).T
    up0, inv0 = up_ref[...], inv_ref[...]
    d1_row, d1_col = diagonal(gb_ref[lanes:, :])
    r_ref[:lanes, :lanes] = up0 * d0_row
    r_ref[lanes:, :lanes] = jnp.zeros((lanes, lanes), F32)
    r01 = dot(inv0, scaled(gb_ref[:lanes, :], d0_col, d1_row), ((1,), (0,)))
    r_ref[:lanes, lanes:] = r01 * d1_row
    rest = scaled(gb_ref[lanes:, :], d1_col, d1_row) - dot(r01, r01, ((0,), (0,)))
    q0 = dot(y_ref[:, :lanes] * (F32(1.0) / d0_row), inv0, ((1,), (1,)))
    q_ref[0] = q0
    q0_copy = pltpu.make_async_copy(q_ref.at[0], q_out.at[:, pl.ds(0, lanes)], sems.at[1])
    q0_copy.start()
    r_copy = pltpu.make_async_copy(r_ref.at[pl.ds(0, lanes)], r_out.at[pl.ds(0, lanes)], sems.at[2])
    r_copy.start()
    y1 = y_ref[:, lanes:] * (F32(1.0) / d1_row) - dot(q0, r01, ((1,), (0,)))
    up1, inv1 = eliminate(rest)
    r_ref[lanes:, lanes:] = up1 * d1_row
    q_ref[1] = dot(y1, inv1, ((1,), (1,)))
    q1_copy = pltpu.make_async_copy(q_ref.at[1], q_out.at[:, pl.ds(lanes, lanes)], sems.at[3])
    q1_copy.start()
    s_copy = pltpu.make_async_copy(r_ref.at[pl.ds(lanes, lanes)], r_out.at[pl.ds(lanes, lanes)], sems.at[4])
    s_copy.start()
    for cp in (y_copy, q0_copy, r_copy, q1_copy, s_copy):
        cp.wait()


def each(count, body):
    if count <= 16:
        for i in range(count):
            body(i)
    else:
        lax.fori_loop(0, count, lambda i, carry: (body(i), carry)[1], 0)


def pieces(rows, devices):
    size = max(8, rows // devices)
    return size, rows // size


def main_kernel(
    n_snp, n_samp,
    g_hbm, b_hbm, y_ref, gb_ref, up_ref, inv_ref, d_ref,
    g_ref, b_ref, part, rs_rx, coded, coded_rx, meta, meta_rx, scores, dose_t,
    cs_tx, cs_rx, ct_tx, ct_rx, y_own, y_tmp, yq, ysc, yq_rx, ysc_rx,
    ga_w, ga_rx, ga_out, gb_w, gb_rx, gb_out,
    in_s, rs_s, rs_r, ex_s, ex_r, mt_s, mt_r, ag_s, ag_r, cs_s, cs_r, ct_s, ct_r,
    yq_s, yq_r, ysc_s, ysc_r, ga_s, ga_r, ha_s, ha_r, gb_s, gb_r, hb_s, hb_r,
):
    snp, samp = lax.axis_index("snp"), lax.axis_index("samp")
    bits = log2(n_snp)
    devices = n_snp * n_samp
    me = samp * n_snp + snp
    words = g_ref.shape[0]
    rows = PLANES * words
    halves, _, lanes = scores.shape
    width = halves * lanes
    chunks = coded.shape[2]
    cwords = words // chunks
    crow = PLANES * cwords
    krow = crow // 2
    per = PLANES // 2
    samples = rows * n_samp
    own_rows = y_own.shape[1]
    bit = lax.rem(snp, 2)

    def copy(src, dst, ssem, rsem, **peer):
        return pltpu.make_async_remote_copy(
            src_ref=src, dst_ref=dst, send_sem=ssem, recv_sem=rsem,
            device_id=peer, device_id_type=MESH,
        )

    def partner(b):
        return snp + (1 << b) * (1 - 2 * ((snp // (1 << b)) % 2))

    def load_b():
        return pltpu.make_async_copy(b_hbm, b_ref, in_s.at[chunks])

    def load_g(c):
        seg = pl.ds(c * cwords, cwords)
        return pltpu.make_async_copy(g_hbm.at[seg], g_ref.at[seg], in_s.at[c])

    load_g(0).start()
    load_b().start()
    for c in range(1, chunks):
        load_g(c).start()
    barrier = pltpu.get_barrier_semaphore()

    def greet(i):
        peer = lax.rem(me + 1 + i, devices)
        pl.semaphore_signal(
            barrier, inc=1, device_id={"samp": peer // n_snp, "snp": lax.rem(peer, n_snp)}, device_id_type=MESH
        )

    each(devices - 1, greet)

    def at(c, side, size):
        return pl.ds(pl.multiple_of(c * crow + side * krow, 16), size)

    def rs_copy(c):
        return copy(part.at[at(c, 1 - bit, krow)], rs_rx.at[pl.ds(c * krow, krow)],
                    rs_s.at[c], rs_r.at[c], snp=partner(0))

    colsum = jnp.zeros((8, width), F32)

    def product(c, side):
        total = jnp.zeros((8, width), F32)
        for i in range(per):
            t = side * per + i
            word = g_ref[c * cwords:(c + 1) * cwords, :]
            dose = (lax.shift_right_logical(word, jnp.full_like(word, 2 * t)) & 3).astype(F32).astype(BF16)
            prod = jnp.dot(dose, b_ref[...], preferred_element_type=F32)
            part[pl.ds(pl.multiple_of(c * crow + t * cwords, 16), cwords), :] = prod
            total = total + prod.reshape(cwords // 8, 8, width).sum(axis=0)
        return total

    with jax.named_scope("load_wait"):
        load_b().wait()
        load_g(0).wait()
    for c in range(chunks):
        if c:
            load_g(c).wait()
        with jax.named_scope("product_sent"):
            colsum = colsum + product(c, 1 - bit)
        if c == 0:
            with jax.named_scope("greeted"):
                pl.semaphore_wait(barrier, devices - 1)
        rs_copy(c).start()
    with jax.named_scope("product_own"):
        for c in range(chunks):
            colsum = colsum + product(c, bit)
    cs_tx[...] = colsum

    def cs_copy(d):
        return copy(cs_tx, cs_rx.at[d], cs_s.at[d], cs_r.at[d], snp=lax.rem(snp + d, n_snp))

    def ct_copy(d):
        return copy(ct_tx, ct_rx.at[d], ct_s.at[d], ct_r.at[d], samp=lax.rem(samp + d, n_samp))

    each(n_snp - 1, lambda i: cs_copy(i + 1).start())

    def ex_copies(b, h, c):
        return (
            copy(coded.at[b - 1, h, c], coded_rx.at[b - 1, h, c], ex_s.at[b - 1, h, c], ex_r.at[b - 1, h, c], snp=partner(b)),
            copy(meta.at[b - 1, h, c], meta_rx.at[b - 1, h, c], mt_s.at[b - 1, h, c], mt_r.at[b - 1, h, c], snp=partner(b)),
        )

    def code(b, h, c):
        block = part[at(c, bit, krow), h * lanes:(h + 1) * lanes]
        mean = jnp.sum(block, axis=0, keepdims=True) * F32(1.0 / krow)
        block = block - mean
        top = jnp.maximum(jnp.max(jnp.abs(block), axis=0, keepdims=True), F32(1e-30))
        coded[b - 1, h, c] = jnp.round(block * (F32(LEVELS) / top)).astype(jnp.int32).astype(jnp.int16)
        first = lax.broadcasted_iota(jnp.int32, (8, lanes), 0) == 0
        meta[b - 1, h, c] = jnp.where(first, top * F32(1.0 / LEVELS), mean)
        for cp in ex_copies(b, h, c):
            cp.start()

    def arrived(b, h, c):
        for cp in ex_copies(b, h, c):
            cp.wait()
        other = coded_rx[b - 1, h, c].astype(jnp.int32).astype(F32) * meta_rx[b - 1, h, c, 0:1, :]
        return part[at(c, bit, krow), h * lanes:(h + 1) * lanes] + (other + meta_rx[b - 1, h, c, 1:2, :])

    def ag_copy(h, c):
        seg = at(c, bit, krow)
        return copy(scores.at[h, seg], scores.at[h, seg], ag_s.at[h, c], ag_r.at[h, c], snp=partner(0))

    for c in range(chunks):
        with jax.named_scope("rs_wait"):
            rs_copy(c).wait()
        seg = at(c, bit, krow)
        part[seg, :] = part[seg, :] + rs_rx[c * krow:(c + 1) * krow, :]
        if bits > 1:
            code(1, 0, c)
    if bits > 1:
        for h in range(1, halves):
            for c in range(chunks):
                code(1, h, c)

    with jax.named_scope("cs_wait"):
        each(n_snp - 1, lambda i: cs_copy(i + 1).wait())
    tot = colsum
    for d in range(1, n_snp):
        tot = tot + cs_rx[d]
    ct_tx[...] = tot
    each(n_samp - 1, lambda i: ct_copy(i + 1).start())
    with jax.named_scope("dose_t"):
        word_t = g_ref[...].T
        for c in range(chunks):
            for t in range(PLANES):
                off = c * crow + t * cwords
                dose_t[:, off:off + cwords] = ((word_t[:, c * cwords:(c + 1) * cwords] >> (2 * t)) & 3).astype(F32).astype(BF16)
    for b in range(2, bits):
        for h in range(halves):
            for c in range(chunks):
                part[at(c, bit, krow), h * lanes:(h + 1) * lanes] = arrived(b - 1, h, c)
                code(b, h, c)
    with jax.named_scope("ct_wait"):
        each(n_samp - 1, lambda i: ct_copy(i + 1).wait())
    for d in range(1, n_samp):
        tot = tot + ct_rx[d]
    center = tot.sum(axis=0, keepdims=True) / F32(samples)

    def finish_scores(h):
        for c in range(chunks):
            seg = at(c, bit, krow)
            if bits > 1:
                total = arrived(bits - 1, h, c)
            else:
                total = part[seg, h * lanes:(h + 1) * lanes]
            scores[h, seg, :] = (total - center[:, h * lanes:(h + 1) * lanes]).astype(BF16)
            ag_copy(h, c).start()

    def gather_scores(h):
        for c in range(chunks):
            ag_copy(h, c).wait()

    inv_root = F32(1.0) / jnp.sqrt(F32(samples))
    last = n_samp - 1
    relay = n_samp >= 4
    mirrored = samp >= n_samp // 2
    place = jnp.where(mirrored, last - samp, samp)
    slots = n_samp - 1

    def y_part(h, owner):
        blk = dose_t[pl.ds(pl.multiple_of(owner * own_rows, 16), own_rows), :]
        return jnp.dot(blk, scores[h], preferred_element_type=F32) * inv_root

    def owner_of(k):
        v = lax.rem(place + jnp.where(place == 0, last - k, jnp.where(k == 0, last, k)), n_samp)
        return jnp.where(mirrored, last - v, v)

    def y_copies(h, k):
        to, slot = owner_of(k), samp
        if relay:
            handed = jnp.logical_and(place == 0, k == 0)
            to = jnp.where(handed, jnp.where(mirrored, last - 1, 1), to)
            slot = jnp.where(handed, to, samp)
        return (
            copy(yq.at[h, k], yq_rx.at[h, slot], yq_s.at[h, k], yq_r.at[h, slot], samp=to),
            copy(ysc.at[h, k], ysc_rx.at[h, slot], ysc_s.at[h, k], ysc_r.at[h, slot], samp=to),
        )

    def y_wait(h, slot):
        copy(yq.at[h, 0], yq_rx.at[h, slot], yq_s.at[h, 0], yq_r.at[h, slot], samp=samp).wait_recv()
        copy(ysc.at[h, 0], ysc_rx.at[h, slot], ysc_s.at[h, 0], ysc_r.at[h, slot], samp=samp).wait_recv()

    def y_decode(h, slot):
        return yq_rx[h, slot].astype(jnp.int32).astype(F32) * ysc_rx[h, slot, 0:1, :]

    def y_send(h, k, block):
        top = jnp.maximum(jnp.max(jnp.abs(block), axis=0, keepdims=True), F32(1e-30))
        yq[h, k] = jnp.round(block * (F32(LEVELS) / top)).astype(jnp.int32).astype(jnp.int16)
        ysc[h, k] = jnp.broadcast_to(top * F32(1.0 / LEVELS), (8, lanes))
        for cp in y_copies(h, k):
            cp.start()

    def y_early(h):
        each(slots - 1 if relay else slots, lambda k: y_send(h, k, y_part(h, owner_of(k))))
        if relay:
            @pl.when(place != 1)
            def _():
                y_send(h, slots - 1, y_part(h, owner_of(slots - 1)))

            @pl.when(place == 1)
            def _():
                y_tmp[h] = y_part(h, owner_of(slots - 1))
        y_own[h] = y_part(h, samp)

    def y_merge(h):
        if relay:
            @pl.when(place == 1)
            def _():
                y_wait(h, samp)
                y_send(h, slots - 1, y_tmp[h] + y_decode(h, samp))

    def y_finish(h):
        def add(i):
            src = lax.rem(samp + 1 + i, n_samp)
            if relay:
                @pl.when(jnp.logical_or(place != 0, src != last - samp))
                def _():
                    y_wait(h, src)
                    y_own[h] = y_own[h] + y_decode(h, src)
            else:
                y_wait(h, src)
                y_own[h] = y_own[h] + y_decode(h, src)

        each(slots, add)
        y_ref[:, h * lanes:(h + 1) * lanes] = y_own[h]

    snp_total = F32(dose_t.shape[0] * n_snp)

    def gram_of(a, b):
        return lax.dot_general(a, b, (((0,), (0,)), ((), ())), precision=HIGH, preferred_element_type=F32) / snp_total

    def all_sum(work, rx, out, s1, r1, s2, r2):
        size, owners = pieces(work.shape[0], devices)

        def peer_of(i):
            return lax.rem(me + 1 + i, devices)

        def piece(i):
            return pl.ds(pl.multiple_of(i * size, 8), size)

        def where_owner(i, body):
            if owners == devices:
                body()
            else:
                pl.when(i < owners)(body)

        def one(i):
            p = peer_of(i)
            return p, copy(work.at[piece(p)], rx.at[me], s1.at[p], r1.at[me], samp=p // n_snp, snp=lax.rem(p, n_snp))

        def two(i):
            p = peer_of(i)
            return p, copy(out.at[piece(me)], out.at[piece(me)], s2.at[p], r2.at[me], samp=p // n_snp, snp=lax.rem(p, n_snp))

        def start():
            def go(i):
                p, cp = one(i)
                where_owner(p, lambda: cp.start())
            each(devices - 1, go)

        def middle():
            def owned():
                rx[me] = work[piece(me), :]

                def got(i):
                    p = peer_of(i)
                    copy(work.at[piece(0)], rx.at[p], s1.at[p], r1.at[p], samp=samp).wait_recv()
                each(devices - 1, got)
                total = lax.fori_loop(1, devices, lambda j, acc: acc + rx[j], rx[0], unroll=devices <= 16)
                out[piece(me), :] = total
                each(devices - 1, lambda i: two(i)[1].start())
            where_owner(me, owned)

        def finish():
            def got(i):
                p = peer_of(i)
                where_owner(p, lambda: copy(out.at[piece(0)], out.at[piece(p)], s2.at[p], r2.at[p], samp=samp).wait_recv())
            each(devices - 1, got)

        def drain():
            def sent(i):
                p, cp = one(i)
                where_owner(p, lambda: cp.wait_send())
            each(devices - 1, sent)
            where_owner(me, lambda: each(devices - 1, lambda i: two(i)[1].wait_send()))

        return start, middle, finish, drain

    a_start, a_middle, a_finish, a_drain = all_sum(ga_w, ga_rx, ga_out, ga_s, ga_r, ha_s, ha_r)
    b_start, b_middle, b_finish, b_drain = all_sum(gb_w, gb_rx, gb_out, gb_s, gb_r, hb_s, hb_r)

    with jax.named_scope("scores_0"):
        finish_scores(0)
        gather_scores(0)
    with jax.named_scope("y_early_0"):
        y_early(0)
    with jax.named_scope("scores_1"):
        finish_scores(1)
        gather_scores(1)
    with jax.named_scope("y_early_1"):
        y_early(1)
    with jax.named_scope("y_merge_0"):
        y_merge(0)
    with jax.named_scope("y_merge_1"):
        y_merge(1)
    with jax.named_scope("y_finish_0"):
        y_finish(0)
    with jax.named_scope("gram_a"):
        ga_w[...] = gram_of(y_own[0], y_own[0])
        a_start()
    with jax.named_scope("gram_a_middle"):
        a_middle()
    with jax.named_scope("y_finish_1"):
        y_finish(1)
    gb_w[:lanes, :] = gram_of(y_own[0], y_own[1])
    gb_w[lanes:, :] = gram_of(y_own[1], y_own[1])
    b_start()
    a_finish()
    d_row, d_col = diagonal(ga_out[...])
    d_ref[...] = jnp.broadcast_to(d_row, d_ref.shape)
    up_ref[...], inv_ref[...] = eliminate(scaled(ga_out[...], d_col, d_row), b_middle)
    b_finish()
    gb_ref[...] = gb_out[...]
    with jax.named_scope("drain"):
        for h in range(halves):
            def sent(k):
                for cp in y_copies(h, k):
                    cp.wait_send()
            each(slots, sent)
        a_drain()
        b_drain()


def per_device(n_snp, n_samp, genotypes, basis_cols):
    words, snps = genotypes.shape
    width = basis_cols.shape[1]
    rows = PLANES * words
    lanes = width // 2
    chunks = max(1, words // 128)
    own = snps // n_samp
    bits = log2(n_snp)
    devices = n_snp * n_samp
    krow = rows // chunks // 2
    steps = max(1, bits - 1)
    vmem = pl.BlockSpec(memory_space=pltpu.VMEM)
    hbm = pl.BlockSpec(memory_space=pltpu.HBM)
    dma = pltpu.SemaphoreType.DMA
    size_a, size_b = pieces(lanes, devices)[0], pieces(width, devices)[0]
    y, gb, up, inv, diag = pl.pallas_call(
        functools.partial(main_kernel, n_snp, n_samp),
        out_shape=(
            pltpu.VMEM((own, width), F32),
            pltpu.VMEM((width, lanes), F32),
            pltpu.VMEM((lanes, lanes), F32),
            pltpu.VMEM((lanes, lanes), F32),
            pltpu.VMEM((8, lanes), F32),
        ),
        in_specs=[hbm, hbm],
        out_specs=(vmem,) * 5,
        scratch_shapes=[
            pltpu.VMEM((words, snps), jnp.int32),
            pltpu.VMEM((snps, width), BF16),
            pltpu.VMEM((rows, width), F32),
            pltpu.VMEM((rows // 2, width), F32),
            pltpu.VMEM((steps, 2, chunks, krow, lanes), jnp.int16),
            pltpu.VMEM((steps, 2, chunks, krow, lanes), jnp.int16),
            pltpu.VMEM((steps, 2, chunks, 8, lanes), F32),
            pltpu.VMEM((steps, 2, chunks, 8, lanes), F32),
            pltpu.VMEM((2, rows, lanes), BF16),
            pltpu.VMEM((snps, rows), BF16),
            pltpu.VMEM((8, width), F32),
            pltpu.VMEM((n_snp, 8, width), F32),
            pltpu.VMEM((8, width), F32),
            pltpu.VMEM((n_samp, 8, width), F32),
            pltpu.VMEM((2, own, lanes), F32),
            pltpu.VMEM((2, own, lanes), F32),
            pltpu.VMEM((2, n_samp, own, lanes), jnp.int16),
            pltpu.VMEM((2, n_samp, 8, lanes), F32),
            pltpu.VMEM((2, n_samp, own, lanes), jnp.int16),
            pltpu.VMEM((2, n_samp, 8, lanes), F32),
            pltpu.VMEM((lanes, lanes), F32),
            pltpu.VMEM((devices, size_a, lanes), F32),
            pltpu.VMEM((lanes, lanes), F32),
            pltpu.VMEM((width, lanes), F32),
            pltpu.VMEM((devices, size_b, lanes), F32),
            pltpu.VMEM((width, lanes), F32),
            dma((chunks + 1,)),
            dma((chunks,)), dma((chunks,)),
            dma((steps, 2, chunks)), dma((steps, 2, chunks)), dma((steps, 2, chunks)), dma((steps, 2, chunks)),
            dma((2, chunks)), dma((2, chunks)),
            dma((n_snp,)), dma((n_snp,)), dma((n_samp,)), dma((n_samp,)),
            dma((2, n_samp)), dma((2, n_samp)), dma((2, n_samp)), dma((2, n_samp)),
            dma((devices,)), dma((devices,)), dma((devices,)), dma((devices,)),
            dma((devices,)), dma((devices,)), dma((devices,)), dma((devices,)),
        ],
        compiler_params=pltpu.CompilerParams(
            collective_id=0, has_side_effects=True, vmem_limit_bytes=60 * 1024 * 1024
        ),
    )(genotypes, basis_cols)
    y, r_factor, q_next = pl.pallas_call(
        factor_kernel,
        out_shape=(
            jax.ShapeDtypeStruct((own, width), F32),
            jax.ShapeDtypeStruct((width, width), F32),
            jax.ShapeDtypeStruct((own, width), F32),
        ),
        in_specs=[vmem] * 5,
        out_specs=(hbm,) * 3,
        scratch_shapes=[
            pltpu.VMEM((width, width), F32),
            pltpu.VMEM((2, own, lanes), F32),
            dma((5,)),
        ],
        compiler_params=pltpu.CompilerParams(vmem_limit_bytes=16 * 1024 * 1024),
    )(gb, up, inv, diag, y)
    layout = (1, 1, own, width)
    return (y.reshape(layout), r_factor, q_next.reshape(layout))


def solution(mesh):
    return jax.shard_map(
        functools.partial(per_device, mesh.shape["snp"], mesh.shape["samp"]),
        mesh=mesh,
        in_specs=(P(("grp", "samp"), "snp"), P(("grp", "snp"), None)),
        out_specs=(
            P(("grp", "snp"), "samp", None, None),
            P("grp", None),
            P(("grp", "snp"), "samp", None, None),
        ),
        check_vma=False,
    )
```

```python
import functools
import jax
import jax.numpy as jnp
from jax import lax
from jax.experimental import pallas as pl
from jax.experimental.pallas import tpu as pltpu
from jax.sharding import PartitionSpec as P

PLANES = 6
MESH = pl.DeviceIdType.MESH
F32 = jnp.float32
BF16 = jnp.bfloat16
HIGH = lax.Precision.HIGHEST
LEVELS = 32767.0


def log2(n):
    bits = n.bit_length() - 1
    assert 1 << bits == n
    return bits


def eliminate(a, pause=None):
    n = a.shape[0]
    groups = n // 8
    lane = lax.broadcasted_iota(jnp.int32, (8, n), 1)
    sub = lax.broadcasted_iota(jnp.int32, (8, n), 0)
    left = [a[8 * g:8 * g + 8, :] for g in range(groups)]
    right = [jnp.where(lane == sub + 8 * g, F32(1.0), F32(0.0)) for g in range(groups)]

    def across(x, j):
        return jnp.broadcast_to(x[:, j:j + 1], (8, n))

    def down(x, s):
        return jnp.broadcast_to(x[s:s + 1, :], (8, n))

    for g0 in range(groups):
        if pause is not None and g0 == groups // 2:
            pause()
        jl, jr = left[g0], right[g0]
        cols = [across(jl, 8 * g0 + i) for i in range(8)]
        up_l, up_r = jl, jr
        for s in range(0, 8, 2):
            c0, c1 = cols[s], cols[s + 1]
            a00, a10, a11 = down(c0, s), down(c0, s + 1), down(c1, s + 1)
            inv_a = F32(1.0) / a00
            inv_det = F32(1.0) / (a00 * a11 - a10 * a10)
            m = a10 * inv_a
            f = a00 * inv_det

            def step(x):
                u, v = down(x, s), down(x, s + 1)
                v = v - m * u
                w1 = v * f
                w0 = u * inv_a - m * w1
                x = x - c0 * w0 - c1 * w1
                return u, v, jnp.where(sub == s, w0, jnp.where(sub == s + 1, w1, x))

            for i in range(s + 2, 8):
                cols[i] = step(cols[i])[2]
            u, v, jl = step(jl)
            up_l = jnp.where(sub == s, u, jnp.where(sub == s + 1, v, up_l))
            u, v, jr = step(jr)
            up_r = jnp.where(sub == s, u, jnp.where(sub == s + 1, v, up_r))
        left[g0], right[g0] = up_l, up_r
        rows_l = [down(jl, i) for i in range(8)]
        rows_r = [down(jr, i) for i in range(8)]
        for g in range(g0 + 1, groups):
            xl, xr = left[g], right[g]
            for i in range(8):
                col = across(left[g], 8 * g0 + i)
                xl = xl - col * rows_l[i]
                xr = xr - col * rows_r[i]
            left[g], right[g] = xl, xr
    ups, invs = [], []
    for g in range(groups):
        diag = jnp.sum(jnp.where(lane == sub + 8 * g, left[g], F32(0.0)), axis=1, keepdims=True)
        scale = F32(1.0) / jnp.sqrt(diag)
        ups.append(jnp.where(lane >= sub + 8 * g, left[g] * scale, F32(0.0)))
        invs.append(right[g] * scale)
    return jnp.concatenate(ups, axis=0), jnp.concatenate(invs, axis=0)


def dot(a, b, dims):
    return lax.dot_general(a, b, (dims, ((), ())), precision=HIGH, preferred_element_type=F32)


def diagonal(block):
    n = block.shape[0]
    on = lax.broadcasted_iota(jnp.int32, (n, n), 0) == lax.broadcasted_iota(jnp.int32, (n, n), 1)
    kept = jnp.where(on, block, F32(0.0))
    row = jnp.sqrt(jnp.sum(kept, axis=0, keepdims=True))
    col = jnp.sqrt(jnp.sum(kept, axis=1, keepdims=True))
    return row, col


def scaled(block, col, row):
    return block * (F32(1.0) / col) * (F32(1.0) / row)


def factor_kernel(gb_ref, up_ref, inv_ref, d_ref, y_ref, y_out, r_out, q_out, r_ref, q_ref, sems):
    lanes = up_ref.shape[0]
    y_copy = pltpu.make_async_copy(y_ref, y_out, sems.at[0])
    y_copy.start()
    d0_row = d_ref[0:1, :]
    d0_col = jnp.broadcast_to(d0_row, (lanes, lanes)).T
    up0, inv0 = up_ref[...], inv_ref[...]
    d1_row, d1_col = diagonal(gb_ref[lanes:, :])
    r_ref[:lanes, :lanes] = up0 * d0_row
    r_ref[lanes:, :lanes] = jnp.zeros((lanes, lanes), F32)
    r01 = dot(inv0, scaled(gb_ref[:lanes, :], d0_col, d1_row), ((1,), (0,)))
    r_ref[:lanes, lanes:] = r01 * d1_row
    rest = scaled(gb_ref[lanes:, :], d1_col, d1_row) - dot(r01, r01, ((0,), (0,)))
    q0 = dot(y_ref[:, :lanes] * (F32(1.0) / d0_row), inv0, ((1,), (1,)))
    q_ref[0] = q0
    q0_copy = pltpu.make_async_copy(q_ref.at[0], q_out.at[:, pl.ds(0, lanes)], sems.at[1])
    q0_copy.start()
    r_copy = pltpu.make_async_copy(r_ref.at[pl.ds(0, lanes)], r_out.at[pl.ds(0, lanes)], sems.at[2])
    r_copy.start()
    y1 = y_ref[:, lanes:] * (F32(1.0) / d1_row) - dot(q0, r01, ((1,), (0,)))
    up1, inv1 = eliminate(rest)
    r_ref[lanes:, lanes:] = up1 * d1_row
    q_ref[1] = dot(y1, inv1, ((1,), (1,)))
    q1_copy = pltpu.make_async_copy(q_ref.at[1], q_out.at[:, pl.ds(lanes, lanes)], sems.at[3])
    q1_copy.start()
    s_copy = pltpu.make_async_copy(r_ref.at[pl.ds(lanes, lanes)], r_out.at[pl.ds(lanes, lanes)], sems.at[4])
    s_copy.start()
    for cp in (y_copy, q0_copy, r_copy, q1_copy, s_copy):
        cp.wait()


def each(count, body):
    if count <= 16:
        for i in range(count):
            body(i)
    else:
        lax.fori_loop(0, count, lambda i, carry: (body(i), carry)[1], 0)


def pieces(rows, devices):
    size = max(8, rows // devices)
    return size, rows // size


def main_kernel(
    n_snp, n_samp,
    g_hbm, b_hbm, y_ref, gb_ref, up_ref, inv_ref, d_ref,
    g_ref, b_ref, part, rs_rx, coded, coded_rx, meta, meta_rx, scores, dose_t,
    cs_tx, cs_rx, ct_tx, ct_rx, y_own, y_tmp, yq, ysc, yq_rx, ysc_rx,
    ga_w, ga_rx, ga_out, gb_w, gb_rx, gb_out,
    in_s, rs_s, rs_r, ex_s, ex_r, mt_s, mt_r, ag_s, ag_r, cs_s, cs_r, ct_s, ct_r,
    yq_s, yq_r, ysc_s, ysc_r, ga_s, ga_r, ha_s, ha_r, gb_s, gb_r, hb_s, hb_r,
):
    snp, samp = lax.axis_index("snp"), lax.axis_index("samp")
    bits = log2(n_snp)
    devices = n_snp * n_samp
    me = samp * n_snp + snp
    words = g_ref.shape[0]
    rows = PLANES * words
    halves, _, lanes = scores.shape
    width = halves * lanes
    chunks = coded.shape[2]
    cwords = words // chunks
    crow = PLANES * cwords
    krow = crow // 2
    per = PLANES // 2
    samples = rows * n_samp
    own_rows = y_own.shape[1]
    bit = lax.rem(snp, 2)

    def copy(src, dst, ssem, rsem, **peer):
        return pltpu.make_async_remote_copy(
            src_ref=src, dst_ref=dst, send_sem=ssem, recv_sem=rsem,
            device_id=peer, device_id_type=MESH,
        )

    def partner(b):
        return snp + (1 << b) * (1 - 2 * ((snp // (1 << b)) % 2))

    def load_b():
        return pltpu.make_async_copy(b_hbm, b_ref, in_s.at[chunks])

    def load_g(c):
        seg = pl.ds(c * cwords, cwords)
        return pltpu.make_async_copy(g_hbm.at[seg], g_ref.at[seg], in_s.at[c])

    load_g(0).start()
    load_b().start()
    for c in range(1, chunks):
        load_g(c).start()
    barrier = pltpu.get_barrier_semaphore()

    def greet(i):
        peer = lax.rem(me + 1 + i, devices)
        pl.semaphore_signal(
            barrier, inc=1, device_id={"samp": peer // n_snp, "snp": lax.rem(peer, n_snp)}, device_id_type=MESH
        )

    each(devices - 1, greet)

    def at(c, side, size):
        return pl.ds(pl.multiple_of(c * crow + side * krow, 16), size)

    def rs_copy(h, c):
        cols = pl.ds(h * lanes, lanes)
        return copy(part.at[at(c, 1 - bit, krow), cols], rs_rx.at[pl.ds(c * krow, krow), cols],
                    rs_s.at[h, c], rs_r.at[h, c], snp=partner(0))

    colsum = jnp.zeros((8, width), F32)

    def product(c, side):
        total = jnp.zeros((8, width), F32)
        for i in range(per):
            t = side * per + i
            word = g_ref[c * cwords:(c + 1) * cwords, :]
            dose = (lax.shift_right_logical(word, jnp.full_like(word, 2 * t)) & 3).astype(F32).astype(BF16)
            prod = jnp.dot(dose, b_ref[...], preferred_element_type=F32)
            part[pl.ds(pl.multiple_of(c * crow + t * cwords, 16), cwords), :] = prod
            total = total + prod.reshape(cwords // 8, 8, width).sum(axis=0)
        return total

    with jax.named_scope("load_wait"):
        load_b().wait()
        load_g(0).wait()
    for c in range(chunks):
        if c:
            load_g(c).wait()
        with jax.named_scope("product_sent"):
            colsum = colsum + product(c, 1 - bit)
        if c == 0:
            with jax.named_scope("greeted"):
                pl.semaphore_wait(barrier, devices - 1)
        for h in range(halves):
            rs_copy(h, c).start()
    with jax.named_scope("product_own"):
        for c in range(chunks):
            colsum = colsum + product(c, bit)
    cs_tx[...] = colsum

    def cs_copy(d):
        return copy(cs_tx, cs_rx.at[d], cs_s.at[d], cs_r.at[d], snp=lax.rem(snp + d, n_snp))

    def ct_copy(d):
        return copy(ct_tx, ct_rx.at[d], ct_s.at[d], ct_r.at[d], samp=lax.rem(samp + d, n_samp))

    each(n_snp - 1, lambda i: cs_copy(i + 1).start())

    def ex_copies(b, h, c):
        return (
            copy(coded.at[b - 1, h, c], coded_rx.at[b - 1, h, c], ex_s.at[b - 1, h, c], ex_r.at[b - 1, h, c], snp=partner(b)),
            copy(meta.at[b - 1, h, c], meta_rx.at[b - 1, h, c], mt_s.at[b - 1, h, c], mt_r.at[b - 1, h, c], snp=partner(b)),
        )

    def code(b, h, c):
        block = part[at(c, bit, krow), h * lanes:(h + 1) * lanes]
        mean = jnp.sum(block, axis=0, keepdims=True) * F32(1.0 / krow)
        block = block - mean
        top = jnp.maximum(jnp.max(jnp.abs(block), axis=0, keepdims=True), F32(1e-30))
        coded[b - 1, h, c] = jnp.round(block * (F32(LEVELS) / top)).astype(jnp.int32).astype(jnp.int16)
        first = lax.broadcasted_iota(jnp.int32, (8, lanes), 0) == 0
        meta[b - 1, h, c] = jnp.where(first, top * F32(1.0 / LEVELS), mean)
        for cp in ex_copies(b, h, c):
            cp.start()

    def arrived(b, h, c):
        for cp in ex_copies(b, h, c):
            cp.wait()
        other = coded_rx[b - 1, h, c].astype(jnp.int32).astype(F32) * meta_rx[b - 1, h, c, 0:1, :]
        return part[at(c, bit, krow), h * lanes:(h + 1) * lanes] + (other + meta_rx[b - 1, h, c, 1:2, :])

    def ag_copy(h, c):
        seg = at(c, bit, krow)
        return copy(scores.at[h, seg], scores.at[h, seg], ag_s.at[h, c], ag_r.at[h, c], snp=partner(0))

    for h in range(halves):
        for c in range(chunks):
            rs_copy(h, c).wait()
            seg, cols = at(c, bit, krow), slice(h * lanes, (h + 1) * lanes)
            part[seg, cols] = part[seg, cols] + rs_rx[c * krow:(c + 1) * krow, cols]
            if bits > 1:
                code(1, h, c)
    with jax.named_scope("cs_wait"):
        each(n_snp - 1, lambda i: cs_copy(i + 1).wait())
    tot = colsum
    for d in range(1, n_snp):
        tot = tot + cs_rx[d]
    ct_tx[...] = tot
    each(n_samp - 1, lambda i: ct_copy(i + 1).start())
    with jax.named_scope("dose_t"):
        word_t = g_ref[...].T
        for c in range(chunks):
            for t in range(PLANES):
                off = c * crow + t * cwords
                dose_t[:, off:off + cwords] = ((word_t[:, c * cwords:(c + 1) * cwords] >> (2 * t)) & 3).astype(F32).astype(BF16)
    for b in range(2, bits):
        for h in range(halves):
            for c in range(chunks):
                part[at(c, bit, krow), h * lanes:(h + 1) * lanes] = arrived(b - 1, h, c)
                code(b, h, c)
    with jax.named_scope("ct_wait"):
        each(n_samp - 1, lambda i: ct_copy(i + 1).wait())
    for d in range(1, n_samp):
        tot = tot + ct_rx[d]
    center = tot.sum(axis=0, keepdims=True) / F32(samples)

    def finish_scores(h):
        for c in range(chunks):
            seg = at(c, bit, krow)
            if bits > 1:
                total = arrived(bits - 1, h, c)
            else:
                total = part[seg, h * lanes:(h + 1) * lanes]
            scores[h, seg, :] = (total - center[:, h * lanes:(h + 1) * lanes]).astype(BF16)
            ag_copy(h, c).start()

    def gather_scores(h):
        for c in range(chunks):
            ag_copy(h, c).wait()

    inv_root = F32(1.0) / jnp.sqrt(F32(samples))
    last = n_samp - 1
    relay = n_samp >= 4
    mirrored = samp >= n_samp // 2
    place = jnp.where(mirrored, last - samp, samp)
    slots = n_samp - 1

    def y_part(h, owner):
        blk = dose_t[pl.ds(pl.multiple_of(owner * own_rows, 16), own_rows), :]
        return jnp.dot(blk, scores[h], preferred_element_type=F32) * inv_root

    def owner_of(k):
        k = jnp.int32(k)
        inner = jnp.where(k == 0, 1, jnp.where(k == 1, last, k))
        v = lax.rem(place + jnp.where(place == 0, last - k, inner), n_samp)
        return jnp.where(mirrored, last - v, v)

    def y_copies(h, k):
        to, slot = owner_of(k), samp
        if relay:
            handed = jnp.logical_and(place == 0, k == 0)
            to = jnp.where(handed, jnp.where(mirrored, last - 1, 1), to)
            slot = jnp.where(handed, to, samp)
        return (
            copy(yq.at[h, k], yq_rx.at[h, slot], yq_s.at[h, k], yq_r.at[h, slot], samp=to),
            copy(ysc.at[h, k], ysc_rx.at[h, slot], ysc_s.at[h, k], ysc_r.at[h, slot], samp=to),
        )

    def y_wait(h, slot):
        copy(yq.at[h, 0], yq_rx.at[h, slot], yq_s.at[h, 0], yq_r.at[h, slot], samp=samp).wait_recv()
        copy(ysc.at[h, 0], ysc_rx.at[h, slot], ysc_s.at[h, 0], ysc_r.at[h, slot], samp=samp).wait_recv()

    def y_decode(h, slot):
        return yq_rx[h, slot].astype(jnp.int32).astype(F32) * ysc_rx[h, slot, 0:1, :]

    def y_send(h, k, block):
        top = jnp.maximum(jnp.max(jnp.abs(block), axis=0, keepdims=True), F32(1e-30))
        yq[h, k] = jnp.round(block * (F32(LEVELS) / top)).astype(jnp.int32).astype(jnp.int16)
        ysc[h, k] = jnp.broadcast_to(top * F32(1.0 / LEVELS), (8, lanes))
        for cp in y_copies(h, k):
            cp.start()

    def y_first(h):
        each(slots - 1 if relay else slots, lambda k: y_send(h, k, y_part(h, owner_of(k))))

    def y_rest(h):
        if relay:
            @pl.when(place != 1)
            def _():
                y_send(h, slots - 1, y_part(h, owner_of(slots - 1)))

            @pl.when(place == 1)
            def _():
                y_tmp[h] = y_part(h, owner_of(slots - 1))
        y_own[h] = y_part(h, samp)

    def y_merge(h):
        if relay:
            @pl.when(place == 1)
            def _():
                y_wait(h, samp)
                y_send(h, slots - 1, y_tmp[h] + y_decode(h, samp))

    def y_finish(h):
        def add(i):
            src = lax.rem(samp + 1 + i, n_samp)
            if relay:
                @pl.when(jnp.logical_or(place != 0, src != last - samp))
                def _():
                    y_wait(h, src)
                    y_own[h] = y_own[h] + y_decode(h, src)
            else:
                y_wait(h, src)
                y_own[h] = y_own[h] + y_decode(h, src)

        each(slots, add)
        y_ref[:, h * lanes:(h + 1) * lanes] = y_own[h]

    snp_total = F32(dose_t.shape[0] * n_snp)

    def gram_of(a, b):
        return lax.dot_general(a, b, (((0,), (0,)), ((), ())), precision=HIGH, preferred_element_type=F32) / snp_total

    def all_sum(work, rx, out, s1, r1, s2, r2):
        size, owners = pieces(work.shape[0], devices)

        def peer_of(i):
            return lax.rem(me + 1 + i, devices)

        def piece(i):
            return pl.ds(pl.multiple_of(i * size, 8), size)

        def where_owner(i, body):
            if owners == devices:
                body()
            else:
                pl.when(i < owners)(body)

        def one(i):
            p = peer_of(i)
            return p, copy(work.at[piece(p)], rx.at[me], s1.at[p], r1.at[me], samp=p // n_snp, snp=lax.rem(p, n_snp))

        def two(i):
            p = peer_of(i)
            return p, copy(out.at[piece(me)], out.at[piece(me)], s2.at[p], r2.at[me], samp=p // n_snp, snp=lax.rem(p, n_snp))

        def start():
            def go(i):
                p, cp = one(i)
                where_owner(p, lambda: cp.start())
            each(devices - 1, go)

        def middle():
            def owned():
                rx[me] = work[piece(me), :]

                def got(i):
                    p = peer_of(i)
                    copy(work.at[piece(0)], rx.at[p], s1.at[p], r1.at[p], samp=samp).wait_recv()
                each(devices - 1, got)
                total = lax.fori_loop(1, devices, lambda j, acc: acc + rx[j], rx[0], unroll=devices <= 16)
                out[piece(me), :] = total
                each(devices - 1, lambda i: two(i)[1].start())
            where_owner(me, owned)

        def finish():
            def got(i):
                p = peer_of(i)
                where_owner(p, lambda: copy(out.at[piece(0)], out.at[piece(p)], s2.at[p], r2.at[p], samp=samp).wait_recv())
            each(devices - 1, got)

        def drain():
            def sent(i):
                p, cp = one(i)
                where_owner(p, lambda: cp.wait_send())
            each(devices - 1, sent)
            where_owner(me, lambda: each(devices - 1, lambda i: two(i)[1].wait_send()))

        return start, middle, finish, drain

    a_start, a_middle, a_finish, a_drain = all_sum(ga_w, ga_rx, ga_out, ga_s, ga_r, ha_s, ha_r)
    b_start, b_middle, b_finish, b_drain = all_sum(gb_w, gb_rx, gb_out, gb_s, gb_r, hb_s, hb_r)

    with jax.named_scope("scores_0"):
        finish_scores(0)
        gather_scores(0)
    with jax.named_scope("y_sent_0"):
        y_first(0)
        y_rest(0)
    with jax.named_scope("scores_1"):
        finish_scores(1)
        y_merge(0)
        gather_scores(1)
    with jax.named_scope("y_sent_1"):
        y_first(1)
        y_rest(1)
    with jax.named_scope("y_kept_0"):
        y_finish(0)
        ga_w[...] = gram_of(y_own[0], y_own[0])
        a_start()
    with jax.named_scope("y_kept_1"):
        y_merge(1)
        a_middle()
        y_finish(1)
    gb_w[:lanes, :] = gram_of(y_own[0], y_own[1])
    gb_w[lanes:, :] = gram_of(y_own[1], y_own[1])
    b_start()
    a_finish()
    b_middle()
    d_row, d_col = diagonal(ga_out[...])
    d_ref[...] = jnp.broadcast_to(d_row, d_ref.shape)
    up_ref[...], inv_ref[...] = eliminate(scaled(ga_out[...], d_col, d_row))
    b_finish()
    gb_ref[...] = gb_out[...]
    with jax.named_scope("drain"):
        for h in range(halves):
            def sent(k):
                for cp in y_copies(h, k):
                    cp.wait_send()
            each(slots, sent)
        a_drain()
        b_drain()


def per_device(n_snp, n_samp, genotypes, basis_cols):
    words, snps = genotypes.shape
    width = basis_cols.shape[1]
    rows = PLANES * words
    lanes = width // 2
    chunks = max(1, words // 128)
    own = snps // n_samp
    bits = log2(n_snp)
    devices = n_snp * n_samp
    krow = rows // chunks // 2
    steps = max(1, bits - 1)
    vmem = pl.BlockSpec(memory_space=pltpu.VMEM)
    hbm = pl.BlockSpec(memory_space=pltpu.HBM)
    dma = pltpu.SemaphoreType.DMA
    size_a, size_b = pieces(lanes, devices)[0], pieces(width, devices)[0]
    y, gb, up, inv, diag = pl.pallas_call(
        functools.partial(main_kernel, n_snp, n_samp),
        out_shape=(
            pltpu.VMEM((own, width), F32),
            pltpu.VMEM((width, lanes), F32),
            pltpu.VMEM((lanes, lanes), F32),
            pltpu.VMEM((lanes, lanes), F32),
            pltpu.VMEM((8, lanes), F32),
        ),
        in_specs=[hbm, hbm],
        out_specs=(vmem,) * 5,
        scratch_shapes=[
            pltpu.VMEM((words, snps), jnp.int32),
            pltpu.VMEM((snps, width), BF16),
            pltpu.VMEM((rows, width), F32),
            pltpu.VMEM((rows // 2, width), F32),
            pltpu.VMEM((steps, 2, chunks, krow, lanes), jnp.int16),
            pltpu.VMEM((steps, 2, chunks, krow, lanes), jnp.int16),
            pltpu.VMEM((steps, 2, chunks, 8, lanes), F32),
            pltpu.VMEM((steps, 2, chunks, 8, lanes), F32),
            pltpu.VMEM((2, rows, lanes), BF16),
            pltpu.VMEM((snps, rows), BF16),
            pltpu.VMEM((8, width), F32),
            pltpu.VMEM((n_snp, 8, width), F32),
            pltpu.VMEM((8, width), F32),
            pltpu.VMEM((n_samp, 8, width), F32),
            pltpu.VMEM((2, own, lanes), F32),
            pltpu.VMEM((2, own, lanes), F32),
            pltpu.VMEM((2, n_samp, own, lanes), jnp.int16),
            pltpu.VMEM((2, n_samp, 8, lanes), F32),
            pltpu.VMEM((2, n_samp, own, lanes), jnp.int16),
            pltpu.VMEM((2, n_samp, 8, lanes), F32),
            pltpu.VMEM((lanes, lanes), F32),
            pltpu.VMEM((devices, size_a, lanes), F32),
            pltpu.VMEM((lanes, lanes), F32),
            pltpu.VMEM((width, lanes), F32),
            pltpu.VMEM((devices, size_b, lanes), F32),
            pltpu.VMEM((width, lanes), F32),
            dma((chunks + 1,)),
            dma((2, chunks)), dma((2, chunks)),
            dma((steps, 2, chunks)), dma((steps, 2, chunks)), dma((steps, 2, chunks)), dma((steps, 2, chunks)),
            dma((2, chunks)), dma((2, chunks)),
            dma((n_snp,)), dma((n_snp,)), dma((n_samp,)), dma((n_samp,)),
            dma((2, n_samp)), dma((2, n_samp)), dma((2, n_samp)), dma((2, n_samp)),
            dma((devices,)), dma((devices,)), dma((devices,)), dma((devices,)),
            dma((devices,)), dma((devices,)), dma((devices,)), dma((devices,)),
        ],
        compiler_params=pltpu.CompilerParams(
            collective_id=0, has_side_effects=True, vmem_limit_bytes=60 * 1024 * 1024
        ),
    )(genotypes, basis_cols)
    y, r_factor, q_next = pl.pallas_call(
        factor_kernel,
        out_shape=(
            jax.ShapeDtypeStruct((own, width), F32),
            jax.ShapeDtypeStruct((width, width), F32),
            jax.ShapeDtypeStruct((own, width), F32),
        ),
        in_specs=[vmem] * 5,
        out_specs=(hbm,) * 3,
        scratch_shapes=[
            pltpu.VMEM((width, width), F32),
            pltpu.VMEM((2, own, lanes), F32),
            dma((5,)),
        ],
        compiler_params=pltpu.CompilerParams(vmem_limit_bytes=16 * 1024 * 1024),
    )(gb, up, inv, diag, y)
    layout = (1, 1, own, width)
    return (y.reshape(layout), r_factor, q_next.reshape(layout))


def solution(mesh):
    return jax.shard_map(
        functools.partial(per_device, mesh.shape["snp"], mesh.shape["samp"]),
        mesh=mesh,
        in_specs=(P(("grp", "samp"), "snp"), P(("grp", "snp"), None)),
        out_specs=(
            P(("grp", "snp"), "samp", None, None),
            P("grp", None),
            P(("grp", "snp"), "samp", None, None),
        ),
        check_vma=False,
    )
```

```python
import functools
import jax
import jax.numpy as jnp
from jax import lax
from jax.experimental import pallas as pl
from jax.experimental.pallas import tpu as pltpu
from jax.sharding import PartitionSpec as P

PLANES = 6
MESH = pl.DeviceIdType.MESH
F32 = jnp.float32
BF16 = jnp.bfloat16
HIGH = lax.Precision.HIGHEST
LEVELS = 32767.0


def log2(n):
    bits = n.bit_length() - 1
    assert 1 << bits == n
    return bits


def eliminate(a, pause=None):
    n = a.shape[0]
    groups = n // 8
    lane = lax.broadcasted_iota(jnp.int32, (8, n), 1)
    sub = lax.broadcasted_iota(jnp.int32, (8, n), 0)
    left = [a[8 * g:8 * g + 8, :] for g in range(groups)]
    right = [jnp.where(lane == sub + 8 * g, F32(1.0), F32(0.0)) for g in range(groups)]

    def across(x, j):
        return jnp.broadcast_to(x[:, j:j + 1], (8, n))

    def down(x, s):
        return jnp.broadcast_to(x[s:s + 1, :], (8, n))

    for g0 in range(groups):
        if pause is not None and g0 == groups // 2:
            pause()
        jl, jr = left[g0], right[g0]
        cols = [across(jl, 8 * g0 + i) for i in range(8)]
        up_l, up_r = jl, jr
        for s in range(0, 8, 2):
            c0, c1 = cols[s], cols[s + 1]
            a00, a10, a11 = down(c0, s), down(c0, s + 1), down(c1, s + 1)
            inv_a = F32(1.0) / a00
            inv_det = F32(1.0) / (a00 * a11 - a10 * a10)
            m = a10 * inv_a
            f = a00 * inv_det

            def step(x):
                u, v = down(x, s), down(x, s + 1)
                v = v - m * u
                w1 = v * f
                w0 = u * inv_a - m * w1
                x = x - c0 * w0 - c1 * w1
                return u, v, jnp.where(sub == s, w0, jnp.where(sub == s + 1, w1, x))

            for i in range(s + 2, 8):
                cols[i] = step(cols[i])[2]
            u, v, jl = step(jl)
            up_l = jnp.where(sub == s, u, jnp.where(sub == s + 1, v, up_l))
            u, v, jr = step(jr)
            up_r = jnp.where(sub == s, u, jnp.where(sub == s + 1, v, up_r))
        left[g0], right[g0] = up_l, up_r
        rows_l = [down(jl, i) for i in range(8)]
        rows_r = [down(jr, i) for i in range(8)]
        for g in range(g0 + 1, groups):
            xl, xr = left[g], right[g]
            for i in range(8):
                col = across(left[g], 8 * g0 + i)
                xl = xl - col * rows_l[i]
                xr = xr - col * rows_r[i]
            left[g], right[g] = xl, xr
    ups, invs = [], []
    for g in range(groups):
        diag = jnp.sum(jnp.where(lane == sub + 8 * g, left[g], F32(0.0)), axis=1, keepdims=True)
        scale = F32(1.0) / jnp.sqrt(diag)
        ups.append(jnp.where(lane >= sub + 8 * g, left[g] * scale, F32(0.0)))
        invs.append(right[g] * scale)
    return jnp.concatenate(ups, axis=0), jnp.concatenate(invs, axis=0)


def dot(a, b, dims):
    return lax.dot_general(a, b, (dims, ((), ())), precision=HIGH, preferred_element_type=F32)


def diagonal(block):
    n = block.shape[0]
    on = lax.broadcasted_iota(jnp.int32, (n, n), 0) == lax.broadcasted_iota(jnp.int32, (n, n), 1)
    kept = jnp.where(on, block, F32(0.0))
    row = jnp.sqrt(jnp.sum(kept, axis=0, keepdims=True))
    col = jnp.sqrt(jnp.sum(kept, axis=1, keepdims=True))
    return row, col


def scaled(block, col, row):
    return block * (F32(1.0) / col) * (F32(1.0) / row)


def factor_kernel(gb_ref, up_ref, inv_ref, d_ref, y_ref, y_out, r_out, q_out, r_ref, q_ref, sems):
    lanes = up_ref.shape[0]
    y_copy = pltpu.make_async_copy(y_ref, y_out, sems.at[0])
    y_copy.start()
    d0_row = d_ref[0:1, :]
    d0_col = jnp.broadcast_to(d0_row, (lanes, lanes)).T
    up0, inv0 = up_ref[...], inv_ref[...]
    d1_row, d1_col = diagonal(gb_ref[lanes:, :])
    r_ref[:lanes, :lanes] = up0 * d0_row
    r_ref[lanes:, :lanes] = jnp.zeros((lanes, lanes), F32)
    r01 = dot(inv0, scaled(gb_ref[:lanes, :], d0_col, d1_row), ((1,), (0,)))
    r_ref[:lanes, lanes:] = r01 * d1_row
    rest = scaled(gb_ref[lanes:, :], d1_col, d1_row) - dot(r01, r01, ((0,), (0,)))
    q0 = dot(y_ref[:, :lanes] * (F32(1.0) / d0_row), inv0, ((1,), (1,)))
    q_ref[0] = q0
    q0_copy = pltpu.make_async_copy(q_ref.at[0], q_out.at[:, pl.ds(0, lanes)], sems.at[1])
    q0_copy.start()
    r_copy = pltpu.make_async_copy(r_ref.at[pl.ds(0, lanes)], r_out.at[pl.ds(0, lanes)], sems.at[2])
    r_copy.start()
    y1 = y_ref[:, lanes:] * (F32(1.0) / d1_row) - dot(q0, r01, ((1,), (0,)))
    up1, inv1 = eliminate(rest)
    r_ref[lanes:, lanes:] = up1 * d1_row
    q_ref[1] = dot(y1, inv1, ((1,), (1,)))
    q1_copy = pltpu.make_async_copy(q_ref.at[1], q_out.at[:, pl.ds(lanes, lanes)], sems.at[3])
    q1_copy.start()
    s_copy = pltpu.make_async_copy(r_ref.at[pl.ds(lanes, lanes)], r_out.at[pl.ds(lanes, lanes)], sems.at[4])
    s_copy.start()
    for cp in (y_copy, q0_copy, r_copy, q1_copy, s_copy):
        cp.wait()


def each(count, body):
    if count <= 16:
        for i in range(count):
            body(i)
    else:
        lax.fori_loop(0, count, lambda i, carry: (body(i), carry)[1], 0)


def pieces(rows, devices):
    size = max(8, rows // devices)
    return size, rows // size


GROUPS = ((0, 0), (0, 1), (1, None))


def lower_lanes(shape):
    return lax.broadcasted_iota(jnp.int32, shape, 1) < shape[1] // 2


def pack(x, side):
    if side is None:
        return x
    n, half = x.shape[0] // 2, x.shape[1] // 2
    top, bottom = x[:n], x[n:]
    if side == 0:
        bottom = pltpu.roll(bottom, half, 1)
    else:
        top = pltpu.roll(top, half, 1)
    return jnp.where(lower_lanes(top.shape), top, bottom)


def unpack(x, side):
    if side is None:
        return x
    other = pltpu.roll(x, x.shape[1] // 2, 1)
    return jnp.concatenate([x, other] if side == 0 else [other, x], axis=0)


def main_kernel(
    n_snp, n_samp,
    g_hbm, b_hbm, y_ref, gb_ref, up_ref, inv_ref, d_ref,
    g_ref, b_ref, part, rs_rx, coded, coded_rx, meta, meta_rx, scores, dose_t,
    cs_tx, cs_rx, y_own, y_tmp, yq, ysc, yq_rx, ysc_rx,
    ga_w, ga_rx, ga_out, gb_w, gb_rx, gb_out,
    in_s, rs_s, rs_r, ex_s, ex_r, mt_s, mt_r, ag_s, ag_r, cs_s, cs_r,
    yq_s, yq_r, ysc_s, ysc_r, ga_s, ga_r, ha_s, ha_r, gb_s, gb_r, hb_s, hb_r,
):
    snp, samp = lax.axis_index("snp"), lax.axis_index("samp")
    bits = log2(n_snp)
    devices = n_snp * n_samp
    me = samp * n_snp + snp
    words = g_ref.shape[0]
    rows = PLANES * words
    groups, _, lanes = scores.shape
    halves = 2
    width = halves * lanes
    chunks = coded.shape[2]
    cwords = words // chunks
    crow = PLANES * cwords
    krow = crow // 2
    per = PLANES // 2
    samples = rows * n_samp
    own_rows = y_own.shape[1]
    bit = lax.rem(snp, 2)

    def copy(src, dst, ssem, rsem, **peer):
        return pltpu.make_async_remote_copy(
            src_ref=src, dst_ref=dst, send_sem=ssem, recv_sem=rsem,
            device_id=peer, device_id_type=MESH,
        )

    def partner(b):
        return snp + (1 << b) * (1 - 2 * ((snp // (1 << b)) % 2))

    def load_b():
        return pltpu.make_async_copy(b_hbm, b_ref, in_s.at[chunks])

    def load_g(c):
        seg = pl.ds(c * cwords, cwords)
        return pltpu.make_async_copy(g_hbm.at[seg], g_ref.at[seg], in_s.at[c])

    load_g(0).start()
    load_b().start()
    for c in range(1, chunks):
        load_g(c).start()
    barrier = pltpu.get_barrier_semaphore()

    def greet(i):
        peer = lax.rem(me + 1 + i, devices)
        pl.semaphore_signal(
            barrier, inc=1, device_id={"samp": peer // n_snp, "snp": lax.rem(peer, n_snp)}, device_id_type=MESH
        )

    each(devices - 1, greet)

    def at(c, side, size):
        return pl.ds(pl.multiple_of(c * crow + side * krow, 16), size)

    def rs_copy(h, c):
        cols = pl.ds(h * lanes, lanes)
        return copy(part.at[at(c, 1 - bit, krow), cols], rs_rx.at[pl.ds(c * krow, krow), cols],
                    rs_s.at[h, c], rs_r.at[h, c], snp=partner(0))

    colsum = jnp.zeros((8, width), F32)

    def product(c, side):
        total = jnp.zeros((8, width), F32)
        for i in range(per):
            t = side * per + i
            word = g_ref[c * cwords:(c + 1) * cwords, :]
            dose = (lax.shift_right_logical(word, jnp.full_like(word, 2 * t)) & 3).astype(F32).astype(BF16)
            prod = jnp.dot(dose, b_ref[...], preferred_element_type=F32)
            part[pl.ds(pl.multiple_of(c * crow + t * cwords, 16), cwords), :] = prod
            total = total + prod.reshape(cwords // 8, 8, width).sum(axis=0)
        return total

    with jax.named_scope("load_wait"):
        load_b().wait()
        load_g(0).wait()
    for c in range(chunks):
        if c:
            load_g(c).wait()
        with jax.named_scope("product_sent"):
            colsum = colsum + product(c, 1 - bit)
        if c == 0:
            with jax.named_scope("greeted"):
                pl.semaphore_wait(barrier, devices - 1)
        for h in range(halves):
            rs_copy(h, c).start()
    with jax.named_scope("product_own"):
        for c in range(chunks):
            colsum = colsum + product(c, bit)
    colsum = jnp.sum(colsum, axis=0, keepdims=True)
    top_row = lax.broadcasted_iota(jnp.int32, (8, lanes), 0) == 0
    cs_tx[...] = jnp.where(top_row, colsum[:, :lanes], colsum[:, lanes:])

    def cs_copy(i):
        p = lax.rem(me + 1 + i, devices)
        return copy(cs_tx, cs_rx.at[me], cs_s.at[p], cs_r.at[me], samp=p // n_snp, snp=lax.rem(p, n_snp))

    def cs_wait(i):
        p = lax.rem(me + 1 + i, devices)
        copy(cs_tx, cs_rx.at[p], cs_s.at[p], cs_r.at[p], samp=samp).wait_recv()

    each(devices - 1, lambda i: cs_copy(i).start())

    def block_at(g, c):
        h = GROUPS[g][0]
        return at(c, bit, krow), slice(h * lanes, (h + 1) * lanes)

    def ex_rows(g):
        return krow if GROUPS[g][1] is None else krow // 2

    def ex_copies(b, g, c):
        seg = pl.ds(0, ex_rows(g))
        return (
            copy(coded.at[b - 1, g, c, seg], coded_rx.at[b - 1, g, c, seg], ex_s.at[b - 1, g, c], ex_r.at[b - 1, g, c], snp=partner(b)),
            copy(meta.at[b - 1, g, c], meta_rx.at[b - 1, g, c], mt_s.at[b - 1, g, c], mt_r.at[b - 1, g, c], snp=partner(b)),
        )

    def code(b, g, c):
        block = pack(part[block_at(g, c)], GROUPS[g][1])
        mean = jnp.sum(block, axis=0, keepdims=True) * F32(1.0 / ex_rows(g))
        block = block - mean
        top = jnp.maximum(jnp.max(jnp.abs(block), axis=0, keepdims=True), F32(1e-30))
        coded[b - 1, g, c, :ex_rows(g), :] = jnp.round(block * (F32(LEVELS) / top)).astype(jnp.int32).astype(jnp.int16)
        first = lax.broadcasted_iota(jnp.int32, (8, lanes), 0) == 0
        meta[b - 1, g, c] = jnp.where(first, top * F32(1.0 / LEVELS), mean)
        for cp in ex_copies(b, g, c):
            cp.start()

    def arrived(b, g, c):
        for cp in ex_copies(b, g, c):
            cp.wait()
        side = GROUPS[g][1]
        other = coded_rx[b - 1, g, c, :ex_rows(g), :].astype(jnp.int32).astype(F32) * meta_rx[b - 1, g, c, 0:1, :]
        other = unpack(other + meta_rx[b - 1, g, c, 1:2, :], side)
        if side is not None:
            low = lower_lanes(other.shape)
            other = jnp.where(low if side == 0 else jnp.logical_not(low), other, F32(0.0))
        return part[block_at(g, c)] + other

    def ag_copy(h, c):
        seg = at(c, bit, krow)
        return copy(scores.at[h, seg], scores.at[h, seg], ag_s.at[h, c], ag_r.at[h, c], snp=partner(0))

    for g in range(groups):
        for c in range(chunks):
            h, side = GROUPS[g]
            if side != 1:
                rs_copy(h, c).wait()
                seg = block_at(g, c)
                part[seg] = part[seg] + rs_rx[c * krow:(c + 1) * krow, h * lanes:(h + 1) * lanes]
            if bits > 1:
                code(1, g, c)
    with jax.named_scope("dose_t"):
        word_t = g_ref[...].T
        for c in range(chunks):
            for t in range(PLANES):
                off = c * crow + t * cwords
                dose_t[:, off:off + cwords] = ((word_t[:, c * cwords:(c + 1) * cwords] >> (2 * t)) & 3).astype(F32).astype(BF16)
    for b in range(2, bits):
        for g in range(groups):
            for c in range(chunks):
                part[block_at(g, c)] = arrived(b - 1, g, c)
                code(b, g, c)
    cs_rx[me] = cs_tx[...]
    with jax.named_scope("center"):
        each(devices - 1, cs_wait)
    tot = lax.fori_loop(1, devices, lambda j, acc: acc + cs_rx[j], cs_rx[0], unroll=devices <= 16)
    center = jnp.concatenate([tot[0:1, :], tot[1:2, :]], axis=1) / F32(samples)

    def finish_scores(g):
        h = GROUPS[g][0]
        for c in range(chunks):
            total = arrived(bits - 1, g, c) if bits > 1 else part[block_at(g, c)]
            scores[g, at(c, bit, krow), :] = (total - center[:, h * lanes:(h + 1) * lanes]).astype(BF16)
            ag_copy(g, c).start()

    def gather_scores(h):
        for c in range(chunks):
            ag_copy(h, c).wait()

    inv_root = F32(1.0) / jnp.sqrt(F32(samples))
    last = n_samp - 1
    relay = n_samp >= 4
    mirrored = samp >= n_samp // 2
    place = jnp.where(mirrored, last - samp, samp)
    slots = n_samp - 1

    def y_part(h, owner):
        blk = dose_t[pl.ds(pl.multiple_of(owner * own_rows, 16), own_rows), :]
        return jnp.dot(blk, scores[h], preferred_element_type=F32) * inv_root

    def owner_of(k):
        k = jnp.int32(k)
        inner = jnp.where(k == 0, 1, jnp.where(k == 1, last, k))
        v = lax.rem(place + jnp.where(place == 0, last - k, inner), n_samp)
        return jnp.where(mirrored, last - v, v)

    def y_rows(h):
        return own_rows if GROUPS[h][1] is None else own_rows // 2

    def y_seg(h):
        return pl.ds(0, y_rows(h))

    def y_copies(h, k):
        to, slot = owner_of(k), samp
        if relay:
            handed = jnp.logical_and(place == 0, k == 0)
            to = jnp.where(handed, jnp.where(mirrored, last - 1, 1), to)
            slot = jnp.where(handed, to, samp)
        return (
            copy(yq.at[h, k, y_seg(h)], yq_rx.at[h, slot, y_seg(h)], yq_s.at[h, k], yq_r.at[h, slot], samp=to),
            copy(ysc.at[h, k], ysc_rx.at[h, slot], ysc_s.at[h, k], ysc_r.at[h, slot], samp=to),
        )

    def y_wait(h, slot):
        copy(yq.at[h, 0, y_seg(h)], yq_rx.at[h, slot, y_seg(h)], yq_s.at[h, 0], yq_r.at[h, slot], samp=samp).wait_recv()
        copy(ysc.at[h, 0], ysc_rx.at[h, slot], ysc_s.at[h, 0], ysc_r.at[h, slot], samp=samp).wait_recv()

    def y_decode(h, slot):
        return yq_rx[h, slot, :y_rows(h), :].astype(jnp.int32).astype(F32) * ysc_rx[h, slot, 0:1, :]

    def y_send(h, k, block):
        top = jnp.maximum(jnp.max(jnp.abs(block), axis=0, keepdims=True), F32(1e-30))
        yq[h, k, :y_rows(h), :] = jnp.round(block * (F32(LEVELS) / top)).astype(jnp.int32).astype(jnp.int16)
        ysc[h, k] = jnp.broadcast_to(top * F32(1.0 / LEVELS), (8, lanes))
        for cp in y_copies(h, k):
            cp.start()

    def y_first(h):
        each(slots - 1 if relay else slots, lambda k: y_send(h, k, pack(y_part(h, owner_of(k)), GROUPS[h][1])))

    def y_rest(h):
        if relay:
            @pl.when(place != 1)
            def _():
                y_send(h, slots - 1, pack(y_part(h, owner_of(slots - 1)), GROUPS[h][1]))

            @pl.when(place == 1)
            def _():
                y_tmp[h, :y_rows(h), :] = pack(y_part(h, owner_of(slots - 1)), GROUPS[h][1])
        y_own[h] = y_part(h, samp)

    def y_merge(h):
        if relay:
            @pl.when(place == 1)
            def _():
                y_wait(h, samp)
                y_send(h, slots - 1, y_tmp[h, :y_rows(h), :] + y_decode(h, samp))

    def y_finish(h):
        def add(i):
            src = lax.rem(samp + 1 + i, n_samp)
            if relay:
                @pl.when(jnp.logical_or(place != 0, src != last - samp))
                def _():
                    y_wait(h, src)
                    y_own[h] = y_own[h] + unpack(y_decode(h, src), GROUPS[h][1])
            else:
                y_wait(h, src)
                y_own[h] = y_own[h] + unpack(y_decode(h, src), GROUPS[h][1])

        each(slots, add)

    snp_total = F32(dose_t.shape[0] * n_snp)

    def gram_of(a, b):
        return lax.dot_general(a, b, (((0,), (0,)), ((), ())), precision=HIGH, preferred_element_type=F32) / snp_total

    def all_sum(work, rx, out, s1, r1, s2, r2):
        size, owners = pieces(work.shape[0], devices)

        def peer_of(i):
            return lax.rem(me + 1 + i, devices)

        def piece(i):
            return pl.ds(pl.multiple_of(i * size, 8), size)

        def where_owner(i, body):
            if owners == devices:
                body()
            else:
                pl.when(i < owners)(body)

        def one(i):
            p = peer_of(i)
            return p, copy(work.at[piece(p)], rx.at[me], s1.at[p], r1.at[me], samp=p // n_snp, snp=lax.rem(p, n_snp))

        def two(i):
            p = peer_of(i)
            return p, copy(out.at[piece(me)], out.at[piece(me)], s2.at[p], r2.at[me], samp=p // n_snp, snp=lax.rem(p, n_snp))

        def start():
            def go(i):
                p, cp = one(i)
                where_owner(p, lambda: cp.start())
            each(devices - 1, go)

        def middle():
            def owned():
                rx[me] = work[piece(me), :]

                def got(i):
                    p = peer_of(i)
                    copy(work.at[piece(0)], rx.at[p], s1.at[p], r1.at[p], samp=samp).wait_recv()
                each(devices - 1, got)
                total = lax.fori_loop(1, devices, lambda j, acc: acc + rx[j], rx[0], unroll=devices <= 16)
                out[piece(me), :] = total
                each(devices - 1, lambda i: two(i)[1].start())
            where_owner(me, owned)

        def finish():
            def got(i):
                p = peer_of(i)
                where_owner(p, lambda: copy(out.at[piece(0)], out.at[piece(p)], s2.at[p], r2.at[p], samp=samp).wait_recv())
            each(devices - 1, got)

        def drain():
            def sent(i):
                p, cp = one(i)
                where_owner(p, lambda: cp.wait_send())
            each(devices - 1, sent)
            where_owner(me, lambda: each(devices - 1, lambda i: two(i)[1].wait_send()))

        return start, middle, finish, drain

    a_start, a_middle, a_finish, a_drain = all_sum(ga_w, ga_rx, ga_out, ga_s, ga_r, ha_s, ha_r)
    b_start, b_middle, b_finish, b_drain = all_sum(gb_w, gb_rx, gb_out, gb_s, gb_r, hb_s, hb_r)

    for g in range(groups):
        with jax.named_scope("scores"):
            finish_scores(g)
            if g:
                y_merge(g - 1)
            gather_scores(g)
        with jax.named_scope("y_sent"):
            y_first(g)
            y_rest(g)
    with jax.named_scope("y_kept"):
        y_finish(0)
        y_finish(1)
        y0 = jnp.where(lower_lanes((own_rows, lanes)), y_own[0], y_own[1])
        y_ref[:, :lanes] = y0
        ga_w[...] = gram_of(y0, y0)
        a_start()
    with jax.named_scope("y_kept_last"):
        y_merge(2)
        a_middle()
        y_finish(2)
        y1 = y_own[2]
        y_ref[:, lanes:] = y1
    gb_w[:lanes, :] = gram_of(y_ref[:, :lanes], y1)
    gb_w[lanes:, :] = gram_of(y1, y1)
    b_start()
    a_finish()
    b_middle()
    d_row, d_col = diagonal(ga_out[...])
    d_ref[...] = jnp.broadcast_to(d_row, d_ref.shape)
    up_ref[...], inv_ref[...] = eliminate(scaled(ga_out[...], d_col, d_row))
    b_finish()
    gb_ref[...] = gb_out[...]
    with jax.named_scope("drain"):
        each(devices - 1, lambda i: cs_copy(i).wait_send())
        for g in range(groups):
            def sent(k):
                for cp in y_copies(g, k):
                    cp.wait_send()
            each(slots, sent)
        a_drain()
        b_drain()


def per_device(n_snp, n_samp, genotypes, basis_cols):
    words, snps = genotypes.shape
    width = basis_cols.shape[1]
    rows = PLANES * words
    lanes = width // 2
    chunks = max(1, words // 128)
    own = snps // n_samp
    bits = log2(n_snp)
    devices = n_snp * n_samp
    krow = rows // chunks // 2
    steps = max(1, bits - 1)
    groups = len(GROUPS)
    vmem = pl.BlockSpec(memory_space=pltpu.VMEM)
    hbm = pl.BlockSpec(memory_space=pltpu.HBM)
    dma = pltpu.SemaphoreType.DMA
    size_a, size_b = pieces(lanes, devices)[0], pieces(width, devices)[0]
    y, gb, up, inv, diag = pl.pallas_call(
        functools.partial(main_kernel, n_snp, n_samp),
        out_shape=(
            pltpu.VMEM((own, width), F32),
            pltpu.VMEM((width, lanes), F32),
            pltpu.VMEM((lanes, lanes), F32),
            pltpu.VMEM((lanes, lanes), F32),
            pltpu.VMEM((8, lanes), F32),
        ),
        in_specs=[hbm, hbm],
        out_specs=(vmem,) * 5,
        scratch_shapes=[
            pltpu.VMEM((words, snps), jnp.int32),
            pltpu.VMEM((snps, width), BF16),
            pltpu.VMEM((rows, width), F32),
            pltpu.VMEM((rows // 2, width), F32),
            pltpu.VMEM((steps, groups, chunks, krow, lanes), jnp.int16),
            pltpu.VMEM((steps, groups, chunks, krow, lanes), jnp.int16),
            pltpu.VMEM((steps, groups, chunks, 8, lanes), F32),
            pltpu.VMEM((steps, groups, chunks, 8, lanes), F32),
            pltpu.VMEM((groups, rows, lanes), BF16),
            pltpu.VMEM((snps, rows), BF16),
            pltpu.VMEM((8, lanes), F32),
            pltpu.VMEM((devices, 8, lanes), F32),
            pltpu.VMEM((groups, own, lanes), F32),
            pltpu.VMEM((groups, own, lanes), F32),
            pltpu.VMEM((groups, n_samp, own, lanes), jnp.int16),
            pltpu.VMEM((groups, n_samp, 8, lanes), F32),
            pltpu.VMEM((groups, n_samp, own, lanes), jnp.int16),
            pltpu.VMEM((groups, n_samp, 8, lanes), F32),
            pltpu.VMEM((lanes, lanes), F32),
            pltpu.VMEM((devices, size_a, lanes), F32),
            pltpu.VMEM((lanes, lanes), F32),
            pltpu.VMEM((width, lanes), F32),
            pltpu.VMEM((devices, size_b, lanes), F32),
            pltpu.VMEM((width, lanes), F32),
            dma((chunks + 1,)),
            dma((2, chunks)), dma((2, chunks)),
            dma((steps, groups, chunks)), dma((steps, groups, chunks)), dma((steps, groups, chunks)), dma((steps, groups, chunks)),
            dma((groups, chunks)), dma((groups, chunks)),
            dma((devices,)), dma((devices,)),
            dma((groups, n_samp)), dma((groups, n_samp)), dma((groups, n_samp)), dma((groups, n_samp)),
            dma((devices,)), dma((devices,)), dma((devices,)), dma((devices,)),
            dma((devices,)), dma((devices,)), dma((devices,)), dma((devices,)),
        ],
        compiler_params=pltpu.CompilerParams(
            collective_id=0, has_side_effects=True, vmem_limit_bytes=60 * 1024 * 1024
        ),
    )(genotypes, basis_cols)
    y, r_factor, q_next = pl.pallas_call(
        factor_kernel,
        out_shape=(
            jax.ShapeDtypeStruct((own, width), F32),
            jax.ShapeDtypeStruct((width, width), F32),
            jax.ShapeDtypeStruct((own, width), F32),
        ),
        in_specs=[vmem] * 5,
        out_specs=(hbm,) * 3,
        scratch_shapes=[
            pltpu.VMEM((width, width), F32),
            pltpu.VMEM((2, own, lanes), F32),
            dma((5,)),
        ],
        compiler_params=pltpu.CompilerParams(vmem_limit_bytes=16 * 1024 * 1024),
    )(gb, up, inv, diag, y)
    layout = (1, 1, own, width)
    return (y.reshape(layout), r_factor, q_next.reshape(layout))


def solution(mesh):
    return jax.shard_map(
        functools.partial(per_device, mesh.shape["snp"], mesh.shape["samp"]),
        mesh=mesh,
        in_specs=(P(("grp", "samp"), "snp"), P(("grp", "snp"), None)),
        out_specs=(
            P(("grp", "snp"), "samp", None, None),
            P("grp", None),
            P(("grp", "snp"), "samp", None, None),
        ),
        check_vma=False,
    )
```

```python
import functools
import jax
import jax.numpy as jnp
from jax import lax
from jax.experimental import pallas as pl
from jax.experimental.pallas import tpu as pltpu
from jax.sharding import PartitionSpec as P

PLANES = 6
MESH = pl.DeviceIdType.MESH
F32 = jnp.float32
BF16 = jnp.bfloat16
HIGH = lax.Precision.HIGHEST
LEVELS = 32767.0


def log2(n):
    bits = n.bit_length() - 1
    assert 1 << bits == n
    return bits


def eliminate(a, pause=None):
    n = a.shape[0]
    groups = n // 8
    lane = lax.broadcasted_iota(jnp.int32, (8, n), 1)
    sub = lax.broadcasted_iota(jnp.int32, (8, n), 0)
    left = [a[8 * g:8 * g + 8, :] for g in range(groups)]
    right = [jnp.where(lane == sub + 8 * g, F32(1.0), F32(0.0)) for g in range(groups)]

    def across(x, j):
        return jnp.broadcast_to(x[:, j:j + 1], (8, n))

    def down(x, s):
        return jnp.broadcast_to(x[s:s + 1, :], (8, n))

    for g0 in range(groups):
        if pause is not None and g0 == groups // 2:
            pause()
        jl, jr = left[g0], right[g0]
        cols = [across(jl, 8 * g0 + i) for i in range(8)]
        up_l, up_r = jl, jr
        for s in range(0, 8, 2):
            c0, c1 = cols[s], cols[s + 1]
            a00, a10, a11 = down(c0, s), down(c0, s + 1), down(c1, s + 1)
            inv_a = F32(1.0) / a00
            inv_det = F32(1.0) / (a00 * a11 - a10 * a10)

            def step(x):
                u, v = down(x, s), down(x, s + 1)
                p0 = a11 * u - a10 * v
                p1 = a00 * v - a10 * u
                taken = jnp.where(sub == s, -p0, jnp.where(sub == s + 1, -p1, c0 * p0 + c1 * p1))
                kept = jnp.where(jnp.logical_or(sub == s, sub == s + 1), F32(0.0), x)
                return u, p1 * inv_a, kept - taken * inv_det

            for i in range(s + 2, 8):
                cols[i] = step(cols[i])[2]
            u, v, jl = step(jl)
            up_l = jnp.where(sub == s, u, jnp.where(sub == s + 1, v, up_l))
            u, v, jr = step(jr)
            up_r = jnp.where(sub == s, u, jnp.where(sub == s + 1, v, up_r))
        left[g0], right[g0] = up_l, up_r
        rows_l = [down(jl, i) for i in range(8)]
        rows_r = [down(jr, i) for i in range(8)]
        for g in range(g0 + 1, groups):
            xl, xr = left[g], right[g]
            for i in range(8):
                col = across(left[g], 8 * g0 + i)
                xl = xl - col * rows_l[i]
                xr = xr - col * rows_r[i]
            left[g], right[g] = xl, xr
    ups, invs = [], []
    for g in range(groups):
        diag = jnp.sum(jnp.where(lane == sub + 8 * g, left[g], F32(0.0)), axis=1, keepdims=True)
        scale = F32(1.0) / jnp.sqrt(diag)
        ups.append(jnp.where(lane >= sub + 8 * g, left[g] * scale, F32(0.0)))
        invs.append(right[g] * scale)
    return jnp.concatenate(ups, axis=0), jnp.concatenate(invs, axis=0)


def dot(a, b, dims):
    return lax.dot_general(a, b, (dims, ((), ())), precision=HIGH, preferred_element_type=F32)


def diagonal(block):
    n = block.shape[0]
    on = lax.broadcasted_iota(jnp.int32, (n, n), 0) == lax.broadcasted_iota(jnp.int32, (n, n), 1)
    kept = jnp.where(on, block, F32(0.0))
    row = jnp.sqrt(jnp.sum(kept, axis=0, keepdims=True))
    col = jnp.sqrt(jnp.sum(kept, axis=1, keepdims=True))
    return row, col


def scaled(block, col, row):
    return block * (F32(1.0) / col) * (F32(1.0) / row)


def factor_kernel(gb_ref, up_ref, inv_ref, d_ref, y_ref, y_out, r_out, q_out, r_ref, q_ref, sems):
    lanes = up_ref.shape[0]
    y_copy = pltpu.make_async_copy(y_ref, y_out, sems.at[0])
    y_copy.start()
    d0_row = d_ref[0:1, :]
    d0_col = jnp.broadcast_to(d0_row, (lanes, lanes)).T
    up0, inv0 = up_ref[...], inv_ref[...]
    d1_row, d1_col = diagonal(gb_ref[lanes:, :])
    r_ref[:lanes, :lanes] = up0 * d0_row
    r_ref[lanes:, :lanes] = jnp.zeros((lanes, lanes), F32)
    r01 = dot(inv0, scaled(gb_ref[:lanes, :], d0_col, d1_row), ((1,), (0,)))
    r_ref[:lanes, lanes:] = r01 * d1_row
    rest = scaled(gb_ref[lanes:, :], d1_col, d1_row) - dot(r01, r01, ((0,), (0,)))
    q0 = dot(y_ref[:, :lanes] * (F32(1.0) / d0_row), inv0, ((1,), (1,)))
    q_ref[0] = q0
    q0_copy = pltpu.make_async_copy(q_ref.at[0], q_out.at[:, pl.ds(0, lanes)], sems.at[1])
    q0_copy.start()
    r_copy = pltpu.make_async_copy(r_ref.at[pl.ds(0, lanes)], r_out.at[pl.ds(0, lanes)], sems.at[2])
    r_copy.start()
    y1 = y_ref[:, lanes:] * (F32(1.0) / d1_row) - dot(q0, r01, ((1,), (0,)))
    up1, inv1 = eliminate(rest)
    r_ref[lanes:, lanes:] = up1 * d1_row
    q_ref[1] = dot(y1, inv1, ((1,), (1,)))
    q1_copy = pltpu.make_async_copy(q_ref.at[1], q_out.at[:, pl.ds(lanes, lanes)], sems.at[3])
    q1_copy.start()
    s_copy = pltpu.make_async_copy(r_ref.at[pl.ds(lanes, lanes)], r_out.at[pl.ds(lanes, lanes)], sems.at[4])
    s_copy.start()
    for cp in (y_copy, q0_copy, r_copy, q1_copy, s_copy):
        cp.wait()


def each(count, body):
    if count <= 16:
        for i in range(count):
            body(i)
    else:
        lax.fori_loop(0, count, lambda i, carry: (body(i), carry)[1], 0)


def pieces(rows, devices):
    size = max(8, rows // devices)
    return size, rows // size


GROUPS = ((0, 0), (0, 1), (1, None))


def lower_lanes(shape):
    return lax.broadcasted_iota(jnp.int32, shape, 1) < shape[1] // 2


def pack(x, side):
    if side is None:
        return x
    n, half = x.shape[0] // 2, x.shape[1] // 2
    top, bottom = x[:n], x[n:]
    if side == 0:
        bottom = pltpu.roll(bottom, half, 1)
    else:
        top = pltpu.roll(top, half, 1)
    return jnp.where(lower_lanes(top.shape), top, bottom)


def unpack(x, side):
    if side is None:
        return x
    other = pltpu.roll(x, x.shape[1] // 2, 1)
    return jnp.concatenate([x, other] if side == 0 else [other, x], axis=0)


def main_kernel(
    n_snp, n_samp,
    g_hbm, b_hbm, y_ref, gb_ref, up_ref, inv_ref, d_ref,
    g_ref, b_ref, part, rs_rx, coded, coded_rx, meta, meta_rx, scores, dose_t,
    cs_tx, cs_rx, y_own, y_tmp, yq, ysc, yq_rx, ysc_rx,
    ga_w, ga_rx, ga_out, gb_w, gb_rx, gb_out,
    in_s, rs_s, rs_r, ex_s, ex_r, mt_s, mt_r, ag_s, ag_r, cs_s, cs_r,
    yq_s, yq_r, ysc_s, ysc_r, ga_s, ga_r, ha_s, ha_r, gb_s, gb_r, hb_s, hb_r,
):
    snp, samp = lax.axis_index("snp"), lax.axis_index("samp")
    bits = log2(n_snp)
    devices = n_snp * n_samp
    me = samp * n_snp + snp
    words = g_ref.shape[0]
    rows = PLANES * words
    groups, _, lanes = scores.shape
    halves = 2
    width = halves * lanes
    chunks = coded.shape[2]
    cwords = words // chunks
    crow = PLANES * cwords
    krow = crow // 2
    per = PLANES // 2
    samples = rows * n_samp
    own_rows = y_own.shape[1]
    bit = lax.rem(snp, 2)

    def copy(src, dst, ssem, rsem, **peer):
        return pltpu.make_async_remote_copy(
            src_ref=src, dst_ref=dst, send_sem=ssem, recv_sem=rsem,
            device_id=peer, device_id_type=MESH,
        )

    def partner(b):
        return snp + (1 << b) * (1 - 2 * ((snp // (1 << b)) % 2))

    def load_b():
        return pltpu.make_async_copy(b_hbm, b_ref, in_s.at[chunks])

    def load_g(c):
        seg = pl.ds(c * cwords, cwords)
        return pltpu.make_async_copy(g_hbm.at[seg], g_ref.at[seg], in_s.at[c])

    load_g(0).start()
    load_b().start()
    for c in range(1, chunks):
        load_g(c).start()
    barrier = pltpu.get_barrier_semaphore()

    def greet(i):
        peer = lax.rem(me + 1 + i, devices)
        pl.semaphore_signal(
            barrier, inc=1, device_id={"samp": peer // n_snp, "snp": lax.rem(peer, n_snp)}, device_id_type=MESH
        )

    each(devices - 1, greet)

    def at(c, side, size):
        return pl.ds(pl.multiple_of(c * crow + side * krow, 16), size)

    def rs_copy(h, c):
        cols = pl.ds(h * lanes, lanes)
        return copy(part.at[at(c, 1 - bit, krow), cols], rs_rx.at[pl.ds(c * krow, krow), cols],
                    rs_s.at[h, c], rs_r.at[h, c], snp=partner(0))

    colsum = jnp.zeros((8, width), F32)

    def product(c, side):
        total = jnp.zeros((8, width), F32)
        for i in range(per):
            t = side * per + i
            word = g_ref[c * cwords:(c + 1) * cwords, :]
            dose = (lax.shift_right_logical(word, jnp.full_like(word, 2 * t)) & 3).astype(F32).astype(BF16)
            prod = jnp.dot(dose, b_ref[...], preferred_element_type=F32)
            part[pl.ds(pl.multiple_of(c * crow + t * cwords, 16), cwords), :] = prod
            total = total + prod.reshape(cwords // 8, 8, width).sum(axis=0)
        return total

    with jax.named_scope("load_wait"):
        load_b().wait()
        load_g(0).wait()
    for c in range(chunks):
        if c:
            load_g(c).wait()
        with jax.named_scope("product_sent"):
            colsum = colsum + product(c, 1 - bit)
        if c == 0:
            with jax.named_scope("greeted"):
                pl.semaphore_wait(barrier, devices - 1)
        for h in range(halves):
            rs_copy(h, c).start()
    with jax.named_scope("product_own"):
        for c in range(chunks):
            colsum = colsum + product(c, bit)
    colsum = jnp.sum(colsum, axis=0, keepdims=True)
    top_row = lax.broadcasted_iota(jnp.int32, (8, lanes), 0) == 0
    cs_tx[...] = jnp.where(top_row, colsum[:, :lanes], colsum[:, lanes:])

    def cs_copy(i):
        p = lax.rem(me + 1 + i, devices)
        return copy(cs_tx, cs_rx.at[me], cs_s.at[p], cs_r.at[me], samp=p // n_snp, snp=lax.rem(p, n_snp))

    def cs_wait(i):
        p = lax.rem(me + 1 + i, devices)
        copy(cs_tx, cs_rx.at[p], cs_s.at[p], cs_r.at[p], samp=samp).wait_recv()

    each(devices - 1, lambda i: cs_copy(i).start())

    def block_at(g, c):
        h = GROUPS[g][0]
        return at(c, bit, krow), slice(h * lanes, (h + 1) * lanes)

    def ex_rows(g):
        return krow if GROUPS[g][1] is None else krow // 2

    def ex_copies(b, g, c):
        seg = pl.ds(0, ex_rows(g))
        return (
            copy(coded.at[b - 1, g, c, seg], coded_rx.at[b - 1, g, c, seg], ex_s.at[b - 1, g, c], ex_r.at[b - 1, g, c], snp=partner(b)),
            copy(meta.at[b - 1, g, c], meta_rx.at[b - 1, g, c], mt_s.at[b - 1, g, c], mt_r.at[b - 1, g, c], snp=partner(b)),
        )

    def code(b, g, c):
        block = pack(part[block_at(g, c)], GROUPS[g][1])
        mean = jnp.sum(block, axis=0, keepdims=True) * F32(1.0 / ex_rows(g))
        block = block - mean
        top = jnp.maximum(jnp.max(jnp.abs(block), axis=0, keepdims=True), F32(1e-30))
        coded[b - 1, g, c, :ex_rows(g), :] = jnp.round(block * (F32(LEVELS) / top)).astype(jnp.int32).astype(jnp.int16)
        first = lax.broadcasted_iota(jnp.int32, (8, lanes), 0) == 0
        meta[b - 1, g, c] = jnp.where(first, top * F32(1.0 / LEVELS), mean)
        for cp in ex_copies(b, g, c):
            cp.start()

    def arrived(b, g, c):
        for cp in ex_copies(b, g, c):
            cp.wait()
        side = GROUPS[g][1]
        other = coded_rx[b - 1, g, c, :ex_rows(g), :].astype(jnp.int32).astype(F32) * meta_rx[b - 1, g, c, 0:1, :]
        other = unpack(other + meta_rx[b - 1, g, c, 1:2, :], side)
        if side is not None:
            low = lower_lanes(other.shape)
            other = jnp.where(low if side == 0 else jnp.logical_not(low), other, F32(0.0))
        return part[block_at(g, c)] + other

    def ag_copy(h, c):
        seg = at(c, bit, krow)
        return copy(scores.at[h, seg], scores.at[h, seg], ag_s.at[h, c], ag_r.at[h, c], snp=partner(0))

    for g in range(groups):
        for c in range(chunks):
            h, side = GROUPS[g]
            if side != 1:
                rs_copy(h, c).wait()
                seg = block_at(g, c)
                part[seg] = part[seg] + rs_rx[c * krow:(c + 1) * krow, h * lanes:(h + 1) * lanes]
            if bits > 1:
                code(1, g, c)
    with jax.named_scope("dose_t"):
        word_t = g_ref[...].T
        for c in range(chunks):
            for t in range(PLANES):
                off = c * crow + t * cwords
                dose_t[:, off:off + cwords] = ((word_t[:, c * cwords:(c + 1) * cwords] >> (2 * t)) & 3).astype(F32).astype(BF16)
    for b in range(2, bits):
        for g in range(groups):
            for c in range(chunks):
                part[block_at(g, c)] = arrived(b - 1, g, c)
                code(b, g, c)
    cs_rx[me] = cs_tx[...]
    with jax.named_scope("center"):
        each(devices - 1, cs_wait)
    tot = lax.fori_loop(1, devices, lambda j, acc: acc + cs_rx[j], cs_rx[0], unroll=devices <= 16)
    center = jnp.concatenate([tot[0:1, :], tot[1:2, :]], axis=1) / F32(samples)

    def finish_scores(g):
        h = GROUPS[g][0]
        for c in range(chunks):
            total = arrived(bits - 1, g, c) if bits > 1 else part[block_at(g, c)]
            scores[g, at(c, bit, krow), :] = (total - center[:, h * lanes:(h + 1) * lanes]).astype(BF16)
            ag_copy(g, c).start()

    def gather_scores(h):
        for c in range(chunks):
            ag_copy(h, c).wait()

    inv_root = F32(1.0) / jnp.sqrt(F32(samples))
    last = n_samp - 1
    relay = n_samp >= 4
    mirrored = samp >= n_samp // 2
    place = jnp.where(mirrored, last - samp, samp)
    slots = n_samp - 1

    def y_part(h, owner):
        blk = dose_t[pl.ds(pl.multiple_of(owner * own_rows, 16), own_rows), :]
        return jnp.dot(blk, scores[h], preferred_element_type=F32) * inv_root

    def owner_of(k):
        k = jnp.int32(k)
        inner = jnp.where(k == 0, 1, jnp.where(k == 1, last, k))
        v = lax.rem(place + jnp.where(place == 0, last - k, inner), n_samp)
        return jnp.where(mirrored, last - v, v)

    def y_rows(h):
        return own_rows if GROUPS[h][1] is None else own_rows // 2

    def y_seg(h):
        return pl.ds(0, y_rows(h))

    def y_copies(h, k):
        to, slot = owner_of(k), samp
        if relay:
            handed = jnp.logical_and(place == 0, k == 0)
            to = jnp.where(handed, jnp.where(mirrored, last - 1, 1), to)
            slot = jnp.where(handed, to, samp)
        return (
            copy(yq.at[h, k, y_seg(h)], yq_rx.at[h, slot, y_seg(h)], yq_s.at[h, k], yq_r.at[h, slot], samp=to),
            copy(ysc.at[h, k], ysc_rx.at[h, slot], ysc_s.at[h, k], ysc_r.at[h, slot], samp=to),
        )

    def y_wait(h, slot):
        copy(yq.at[h, 0, y_seg(h)], yq_rx.at[h, slot, y_seg(h)], yq_s.at[h, 0], yq_r.at[h, slot], samp=samp).wait_recv()
        copy(ysc.at[h, 0], ysc_rx.at[h, slot], ysc_s.at[h, 0], ysc_r.at[h, slot], samp=samp).wait_recv()

    def y_decode(h, slot):
        return yq_rx[h, slot, :y_rows(h), :].astype(jnp.int32).astype(F32) * ysc_rx[h, slot, 0:1, :]

    def y_send(h, k, block):
        top = jnp.maximum(jnp.max(jnp.abs(block), axis=0, keepdims=True), F32(1e-30))
        yq[h, k, :y_rows(h), :] = jnp.round(block * (F32(LEVELS) / top)).astype(jnp.int32).astype(jnp.int16)
        ysc[h, k] = jnp.broadcast_to(top * F32(1.0 / LEVELS), (8, lanes))
        for cp in y_copies(h, k):
            cp.start()

    def y_first(h):
        each(slots - 1 if relay else slots, lambda k: y_send(h, k, pack(y_part(h, owner_of(k)), GROUPS[h][1])))

    def y_rest(h):
        if relay:
            @pl.when(place != 1)
            def _():
                y_send(h, slots - 1, pack(y_part(h, owner_of(slots - 1)), GROUPS[h][1]))

            @pl.when(place == 1)
            def _():
                y_tmp[h, :y_rows(h), :] = pack(y_part(h, owner_of(slots - 1)), GROUPS[h][1])
        y_own[h] = y_part(h, samp)

    def y_merge(h):
        if relay:
            @pl.when(place == 1)
            def _():
                y_wait(h, samp)
                y_send(h, slots - 1, y_tmp[h, :y_rows(h), :] + y_decode(h, samp))

    def y_finish(h):
        def add(i):
            src = lax.rem(samp + 1 + i, n_samp)
            if relay:
                @pl.when(jnp.logical_or(place != 0, src != last - samp))
                def _():
                    y_wait(h, src)
                    y_own[h] = y_own[h] + unpack(y_decode(h, src), GROUPS[h][1])
            else:
                y_wait(h, src)
                y_own[h] = y_own[h] + unpack(y_decode(h, src), GROUPS[h][1])

        each(slots, add)

    snp_total = F32(dose_t.shape[0] * n_snp)

    def gram_of(a, b):
        return lax.dot_general(a, b, (((0,), (0,)), ((), ())), precision=HIGH, preferred_element_type=F32) / snp_total

    def all_sum(work, rx, out, s1, r1, s2, r2):
        size, owners = pieces(work.shape[0], devices)

        def peer_of(i):
            return lax.rem(me + 1 + i, devices)

        def piece(i):
            return pl.ds(pl.multiple_of(i * size, 8), size)

        def where_owner(i, body):
            if owners == devices:
                body()
            else:
                pl.when(i < owners)(body)

        def one(i):
            p = peer_of(i)
            return p, copy(work.at[piece(p)], rx.at[me], s1.at[p], r1.at[me], samp=p // n_snp, snp=lax.rem(p, n_snp))

        def two(i):
            p = peer_of(i)
            return p, copy(out.at[piece(me)], out.at[piece(me)], s2.at[p], r2.at[me], samp=p // n_snp, snp=lax.rem(p, n_snp))

        def start():
            def go(i):
                p, cp = one(i)
                where_owner(p, lambda: cp.start())
            each(devices - 1, go)

        def middle():
            def owned():
                rx[me] = work[piece(me), :]

                def got(i):
                    p = peer_of(i)
                    copy(work.at[piece(0)], rx.at[p], s1.at[p], r1.at[p], samp=samp).wait_recv()
                each(devices - 1, got)
                total = lax.fori_loop(1, devices, lambda j, acc: acc + rx[j], rx[0], unroll=devices <= 16)
                out[piece(me), :] = total
                each(devices - 1, lambda i: two(i)[1].start())
            where_owner(me, owned)

        def finish():
            def got(i):
                p = peer_of(i)
                where_owner(p, lambda: copy(out.at[piece(0)], out.at[piece(p)], s2.at[p], r2.at[p], samp=samp).wait_recv())
            each(devices - 1, got)

        def drain():
            def sent(i):
                p, cp = one(i)
                where_owner(p, lambda: cp.wait_send())
            each(devices - 1, sent)
            where_owner(me, lambda: each(devices - 1, lambda i: two(i)[1].wait_send()))

        return start, middle, finish, drain

    a_start, a_middle, a_finish, a_drain = all_sum(ga_w, ga_rx, ga_out, ga_s, ga_r, ha_s, ha_r)
    b_start, b_middle, b_finish, b_drain = all_sum(gb_w, gb_rx, gb_out, gb_s, gb_r, hb_s, hb_r)

    for g in range(groups):
        with jax.named_scope("scores"):
            if g == 0:
                finish_scores(g)
            if g:
                y_merge(g - 1)
            gather_scores(g)
        with jax.named_scope("y_sent"):
            y_first(g)
            y_rest(g)
            if g + 1 < groups:
                finish_scores(g + 1)
    with jax.named_scope("y_kept"):
        y_finish(0)
        y_finish(1)
        y0 = jnp.where(lower_lanes((own_rows, lanes)), y_own[0], y_own[1])
        y_ref[:, :lanes] = y0
        ga_w[...] = gram_of(y0, y0)
        a_start()
    with jax.named_scope("y_kept_last"):
        y_merge(2)
        a_middle()
        y_finish(2)
        y1 = y_own[2]
        y_ref[:, lanes:] = y1
    gb_w[:lanes, :] = gram_of(y_ref[:, :lanes], y1)
    gb_w[lanes:, :] = gram_of(y1, y1)
    b_start()
    b_middle()
    a_finish()
    d_row, d_col = diagonal(ga_out[...])
    d_ref[...] = jnp.broadcast_to(d_row, d_ref.shape)
    up_ref[...], inv_ref[...] = eliminate(scaled(ga_out[...], d_col, d_row))
    b_finish()
    gb_ref[...] = gb_out[...]
    with jax.named_scope("drain"):
        each(devices - 1, lambda i: cs_copy(i).wait_send())
        for g in range(groups):
            def sent(k):
                for cp in y_copies(g, k):
                    cp.wait_send()
            each(slots, sent)
        a_drain()
        b_drain()


def per_device(n_snp, n_samp, genotypes, basis_cols):
    words, snps = genotypes.shape
    width = basis_cols.shape[1]
    rows = PLANES * words
    lanes = width // 2
    chunks = max(1, words // 128)
    own = snps // n_samp
    bits = log2(n_snp)
    devices = n_snp * n_samp
    krow = rows // chunks // 2
    steps = max(1, bits - 1)
    groups = len(GROUPS)
    vmem = pl.BlockSpec(memory_space=pltpu.VMEM)
    hbm = pl.BlockSpec(memory_space=pltpu.HBM)
    dma = pltpu.SemaphoreType.DMA
    size_a, size_b = pieces(lanes, devices)[0], pieces(width, devices)[0]
    y, gb, up, inv, diag = pl.pallas_call(
        functools.partial(main_kernel, n_snp, n_samp),
        out_shape=(
            pltpu.VMEM((own, width), F32),
            pltpu.VMEM((width, lanes), F32),
            pltpu.VMEM((lanes, lanes), F32),
            pltpu.VMEM((lanes, lanes), F32),
            pltpu.VMEM((8, lanes), F32),
        ),
        in_specs=[hbm, hbm],
        out_specs=(vmem,) * 5,
        scratch_shapes=[
            pltpu.VMEM((words, snps), jnp.int32),
            pltpu.VMEM((snps, width), BF16),
            pltpu.VMEM((rows, width), F32),
            pltpu.VMEM((rows // 2, width), F32),
            pltpu.VMEM((steps, groups, chunks, krow, lanes), jnp.int16),
            pltpu.VMEM((steps, groups, chunks, krow, lanes), jnp.int16),
            pltpu.VMEM((steps, groups, chunks, 8, lanes), F32),
            pltpu.VMEM((steps, groups, chunks, 8, lanes), F32),
            pltpu.VMEM((groups, rows, lanes), BF16),
            pltpu.VMEM((snps, rows), BF16),
            pltpu.VMEM((8, lanes), F32),
            pltpu.VMEM((devices, 8, lanes), F32),
            pltpu.VMEM((groups, own, lanes), F32),
            pltpu.VMEM((groups, own, lanes), F32),
            pltpu.VMEM((groups, n_samp, own, lanes), jnp.int16),
            pltpu.VMEM((groups, n_samp, 8, lanes), F32),
            pltpu.VMEM((groups, n_samp, own, lanes), jnp.int16),
            pltpu.VMEM((groups, n_samp, 8, lanes), F32),
            pltpu.VMEM((lanes, lanes), F32),
            pltpu.VMEM((devices, size_a, lanes), F32),
            pltpu.VMEM((lanes, lanes), F32),
            pltpu.VMEM((width, lanes), F32),
            pltpu.VMEM((devices, size_b, lanes), F32),
            pltpu.VMEM((width, lanes), F32),
            dma((chunks + 1,)),
            dma((2, chunks)), dma((2, chunks)),
            dma((steps, groups, chunks)), dma((steps, groups, chunks)), dma((steps, groups, chunks)), dma((steps, groups, chunks)),
            dma((groups, chunks)), dma((groups, chunks)),
            dma((devices,)), dma((devices,)),
            dma((groups, n_samp)), dma((groups, n_samp)), dma((groups, n_samp)), dma((groups, n_samp)),
            dma((devices,)), dma((devices,)), dma((devices,)), dma((devices,)),
            dma((devices,)), dma((devices,)), dma((devices,)), dma((devices,)),
        ],
        compiler_params=pltpu.CompilerParams(
            collective_id=0, has_side_effects=True, vmem_limit_bytes=60 * 1024 * 1024
        ),
    )(genotypes, basis_cols)
    y, r_factor, q_next = pl.pallas_call(
        factor_kernel,
        out_shape=(
            jax.ShapeDtypeStruct((own, width), F32),
            jax.ShapeDtypeStruct((width, width), F32),
            jax.ShapeDtypeStruct((own, width), F32),
        ),
        in_specs=[vmem] * 5,
        out_specs=(hbm,) * 3,
        scratch_shapes=[
            pltpu.VMEM((width, width), F32),
            pltpu.VMEM((2, own, lanes), F32),
            dma((5,)),
        ],
        compiler_params=pltpu.CompilerParams(vmem_limit_bytes=16 * 1024 * 1024),
    )(gb, up, inv, diag, y)
    layout = (1, 1, own, width)
    return (y.reshape(layout), r_factor, q_next.reshape(layout))


def solution(mesh):
    return jax.shard_map(
        functools.partial(per_device, mesh.shape["snp"], mesh.shape["samp"]),
        mesh=mesh,
        in_specs=(P(("grp", "samp"), "snp"), P(("grp", "snp"), None)),
        out_specs=(
            P(("grp", "snp"), "samp", None, None),
            P("grp", None),
            P(("grp", "snp"), "samp", None, None),
        ),
        check_vma=False,
    )
```

```python
import functools
import jax
import jax.numpy as jnp
from jax import lax
from jax.experimental import pallas as pl
from jax.experimental.pallas import tpu as pltpu
from jax.sharding import PartitionSpec as P

PLANES = 6
MESH = pl.DeviceIdType.MESH
F32 = jnp.float32
BF16 = jnp.bfloat16
HIGH = lax.Precision.HIGHEST
LEVELS = 32767.0


def log2(n):
    bits = n.bit_length() - 1
    assert 1 << bits == n
    return bits


def eliminate(a, pause=None):
    n = a.shape[0]
    groups = n // 8
    lane = lax.broadcasted_iota(jnp.int32, (8, n), 1)
    sub = lax.broadcasted_iota(jnp.int32, (8, n), 0)
    left = [a[8 * g:8 * g + 8, :] for g in range(groups)]
    right = [jnp.where(lane == sub + 8 * g, F32(1.0), F32(0.0)) for g in range(groups)]

    def across(x, j):
        return jnp.broadcast_to(x[:, j:j + 1], (8, n))

    def down(x, s):
        return jnp.broadcast_to(x[s:s + 1, :], (8, n))

    for g0 in range(groups):
        if pause is not None and g0 == groups // 2:
            pause()
        jl, jr = left[g0], right[g0]
        cols = [across(jl, 8 * g0 + i) for i in range(8)]
        up_l, up_r = jl, jr
        for s in range(0, 8, 2):
            c0, c1 = cols[s], cols[s + 1]
            a00, a10, a11 = down(c0, s), down(c0, s + 1), down(c1, s + 1)
            first, second = sub == s, sub == s + 1
            e0 = jnp.where(first, F32(-1.0), jnp.where(second, F32(0.0), c0))
            e1 = jnp.where(second, F32(-1.0), jnp.where(first, F32(0.0), c1))
            pivot = jnp.logical_or(first, second)
            inv_a = F32(1.0) / a00
            inv_det = F32(1.0) / (a00 * a11 - a10 * a10)

            def step(x):
                u, v = down(x, s), down(x, s + 1)
                p0 = a11 * u - a10 * v
                p1 = a00 * v - a10 * u
                return u, p1 * inv_a, jnp.where(pivot, F32(0.0), x) - (e0 * p0 + e1 * p1) * inv_det

            for i in range(s + 2, 8):
                cols[i] = step(cols[i])[2]
            u, v, jl = step(jl)
            up_l = jnp.where(sub == s, u, jnp.where(sub == s + 1, v, up_l))
            u, v, jr = step(jr)
            up_r = jnp.where(sub == s, u, jnp.where(sub == s + 1, v, up_r))
        left[g0], right[g0] = up_l, up_r
        rows_l = [down(jl, i) for i in range(8)]
        rows_r = [down(jr, i) for i in range(8)]
        for g in range(g0 + 1, groups):
            xl, xr = left[g], right[g]
            for i in range(8):
                col = across(left[g], 8 * g0 + i)
                xl = xl - col * rows_l[i]
                xr = xr - col * rows_r[i]
            left[g], right[g] = xl, xr
    ups, invs = [], []
    for g in range(groups):
        diag = jnp.sum(jnp.where(lane == sub + 8 * g, left[g], F32(0.0)), axis=1, keepdims=True)
        scale = F32(1.0) / jnp.sqrt(diag)
        ups.append(jnp.where(lane >= sub + 8 * g, left[g] * scale, F32(0.0)))
        invs.append(right[g] * scale)
    return jnp.concatenate(ups, axis=0), jnp.concatenate(invs, axis=0)


def dot(a, b, dims):
    return lax.dot_general(a, b, (dims, ((), ())), precision=HIGH, preferred_element_type=F32)


def diagonal(block):
    n = block.shape[0]
    on = lax.broadcasted_iota(jnp.int32, (n, n), 0) == lax.broadcasted_iota(jnp.int32, (n, n), 1)
    kept = jnp.where(on, block, F32(0.0))
    row = jnp.sqrt(jnp.sum(kept, axis=0, keepdims=True))
    col = jnp.sqrt(jnp.sum(kept, axis=1, keepdims=True))
    return row, col


def scaled(block, col, row):
    return block * (F32(1.0) / col) * (F32(1.0) / row)


def factor_kernel(gb_ref, up_ref, inv_ref, d_ref, y_ref, y_out, r_out, q_out, r_ref, q_ref, sems):
    lanes = up_ref.shape[0]
    y_copy = pltpu.make_async_copy(y_ref, y_out, sems.at[0])
    y_copy.start()
    d0_row = d_ref[0:1, :]
    d0_col = jnp.broadcast_to(d0_row, (lanes, lanes)).T
    up0, inv0 = up_ref[...], inv_ref[...]
    d1_row, d1_col = diagonal(gb_ref[lanes:, :])
    r_ref[:lanes, :lanes] = up0 * d0_row
    r_ref[lanes:, :lanes] = jnp.zeros((lanes, lanes), F32)
    r01 = dot(inv0, scaled(gb_ref[:lanes, :], d0_col, d1_row), ((1,), (0,)))
    r_ref[:lanes, lanes:] = r01 * d1_row
    rest = scaled(gb_ref[lanes:, :], d1_col, d1_row) - dot(r01, r01, ((0,), (0,)))
    q0 = dot(y_ref[:, :lanes] * (F32(1.0) / d0_row), inv0, ((1,), (1,)))
    q_ref[0] = q0
    q0_copy = pltpu.make_async_copy(q_ref.at[0], q_out.at[:, pl.ds(0, lanes)], sems.at[1])
    q0_copy.start()
    r_copy = pltpu.make_async_copy(r_ref.at[pl.ds(0, lanes)], r_out.at[pl.ds(0, lanes)], sems.at[2])
    r_copy.start()
    y1 = y_ref[:, lanes:] * (F32(1.0) / d1_row) - dot(q0, r01, ((1,), (0,)))
    up1, inv1 = eliminate(rest)
    r_ref[lanes:, lanes:] = up1 * d1_row
    s_copy = pltpu.make_async_copy(r_ref.at[pl.ds(lanes, lanes)], r_out.at[pl.ds(lanes, lanes)], sems.at[4])
    s_copy.start()
    half = y1.shape[0] // 2
    q1_copies = []
    for i in range(2):
        seg = pl.ds(i * half, half)
        q_ref[1, i * half:(i + 1) * half, :] = dot(y1[i * half:(i + 1) * half], inv1, ((1,), (1,)))
        q1_copies.append(pltpu.make_async_copy(q_ref.at[1, seg], q_out.at[seg, pl.ds(lanes, lanes)], sems.at[3 + 2 * i]))
        q1_copies[i].start()
    for cp in (y_copy, q0_copy, r_copy, s_copy, *q1_copies):
        cp.wait()


def each(count, body):
    if count <= 16:
        for i in range(count):
            body(i)
    else:
        lax.fori_loop(0, count, lambda i, carry: (body(i), carry)[1], 0)


def pieces(rows, devices):
    size = max(8, rows // devices)
    return size, rows // size


GROUPS = ((0, 0), (0, 1), (1, None))


def lower_lanes(shape):
    return lax.broadcasted_iota(jnp.int32, shape, 1) < shape[1] // 2


def pack(x, side):
    if side is None:
        return x
    n, half = x.shape[0] // 2, x.shape[1] // 2
    top, bottom = x[:n], x[n:]
    if side == 0:
        bottom = pltpu.roll(bottom, half, 1)
    else:
        top = pltpu.roll(top, half, 1)
    return jnp.where(lower_lanes(top.shape), top, bottom)


def unpack(x, side):
    if side is None:
        return x
    other = pltpu.roll(x, x.shape[1] // 2, 1)
    return jnp.concatenate([x, other] if side == 0 else [other, x], axis=0)


def main_kernel(
    n_snp, n_samp,
    g_hbm, b_hbm, y_ref, gb_ref, up_ref, inv_ref, d_ref,
    g_ref, b_ref, part, rs_rx, coded, coded_rx, meta, meta_rx, scores, dose_t,
    cs_tx, cs_rx, y_own, y_tmp, yq, ysc, yq_rx, ysc_rx,
    ga_w, ga_rx, ga_out, gb_w, gb_rx, gb_out,
    in_s, rs_s, rs_r, ex_s, ex_r, mt_s, mt_r, ag_s, ag_r, cs_s, cs_r,
    yq_s, yq_r, ysc_s, ysc_r, ga_s, ga_r, ha_s, ha_r, gb_s, gb_r, hb_s, hb_r,
):
    snp, samp = lax.axis_index("snp"), lax.axis_index("samp")
    bits = log2(n_snp)
    devices = n_snp * n_samp
    me = samp * n_snp + snp
    words = g_ref.shape[0]
    rows = PLANES * words
    groups, _, lanes = scores.shape
    halves = 2
    width = halves * lanes
    chunks = coded.shape[2]
    cwords = words // chunks
    crow = PLANES * cwords
    krow = crow // 2
    per = PLANES // 2
    samples = rows * n_samp
    own_rows = y_own.shape[1]
    bit = lax.rem(snp, 2)

    def copy(src, dst, ssem, rsem, **peer):
        return pltpu.make_async_remote_copy(
            src_ref=src, dst_ref=dst, send_sem=ssem, recv_sem=rsem,
            device_id=peer, device_id_type=MESH,
        )

    def partner(b):
        return snp + (1 << b) * (1 - 2 * ((snp // (1 << b)) % 2))

    def load_b():
        return pltpu.make_async_copy(b_hbm, b_ref, in_s.at[chunks])

    def load_g(c):
        seg = pl.ds(c * cwords, cwords)
        return pltpu.make_async_copy(g_hbm.at[seg], g_ref.at[seg], in_s.at[c])

    load_g(0).start()
    load_b().start()
    for c in range(1, chunks):
        load_g(c).start()
    barrier = pltpu.get_barrier_semaphore()

    def greet(i):
        peer = lax.rem(me + 1 + i, devices)
        pl.semaphore_signal(
            barrier, inc=1, device_id={"samp": peer // n_snp, "snp": lax.rem(peer, n_snp)}, device_id_type=MESH
        )

    each(devices - 1, greet)

    def at(c, side, size):
        return pl.ds(pl.multiple_of(c * crow + side * krow, 16), size)

    def rs_copy(h, c):
        cols = pl.ds(h * lanes, lanes)
        return copy(part.at[at(c, 1 - bit, krow), cols], rs_rx.at[pl.ds(c * krow, krow), cols],
                    rs_s.at[h, c], rs_r.at[h, c], snp=partner(0))

    colsum = jnp.zeros((8, width), F32)

    def product(c, side):
        total = jnp.zeros((8, width), F32)
        for i in range(per):
            t = side * per + i
            word = g_ref[c * cwords:(c + 1) * cwords, :]
            dose = (lax.shift_right_logical(word, jnp.full_like(word, 2 * t)) & 3).astype(F32).astype(BF16)
            prod = jnp.dot(dose, b_ref[...], preferred_element_type=F32)
            part[pl.ds(pl.multiple_of(c * crow + t * cwords, 16), cwords), :] = prod
            total = total + prod.reshape(cwords // 8, 8, width).sum(axis=0)
        return total

    with jax.named_scope("load_wait"):
        load_b().wait()
        load_g(0).wait()
    for c in range(chunks):
        if c:
            load_g(c).wait()
        with jax.named_scope("product_sent"):
            colsum = colsum + product(c, 1 - bit)
        if c == 0:
            with jax.named_scope("greeted"):
                pl.semaphore_wait(barrier, devices - 1)
        for h in range(halves):
            rs_copy(h, c).start()
    with jax.named_scope("product_own"):
        for c in range(chunks):
            colsum = colsum + product(c, bit)
    colsum = jnp.sum(colsum, axis=0, keepdims=True)
    top_row = lax.broadcasted_iota(jnp.int32, (8, lanes), 0) == 0
    cs_tx[...] = jnp.where(top_row, colsum[:, :lanes], colsum[:, lanes:])

    def cs_copy(i):
        p = lax.rem(me + 1 + i, devices)
        return copy(cs_tx, cs_rx.at[me], cs_s.at[p], cs_r.at[me], samp=p // n_snp, snp=lax.rem(p, n_snp))

    def cs_wait(i):
        p = lax.rem(me + 1 + i, devices)
        copy(cs_tx, cs_rx.at[p], cs_s.at[p], cs_r.at[p], samp=samp).wait_recv()

    each(devices - 1, lambda i: cs_copy(i).start())

    def block_at(g, c):
        h = GROUPS[g][0]
        return at(c, bit, krow), slice(h * lanes, (h + 1) * lanes)

    def ex_rows(g):
        return krow if GROUPS[g][1] is None else krow // 2

    def ex_copies(b, g, c):
        seg = pl.ds(0, ex_rows(g))
        return (
            copy(coded.at[b - 1, g, c, seg], coded_rx.at[b - 1, g, c, seg], ex_s.at[b - 1, g, c], ex_r.at[b - 1, g, c], snp=partner(b)),
            copy(meta.at[b - 1, g, c], meta_rx.at[b - 1, g, c], mt_s.at[b - 1, g, c], mt_r.at[b - 1, g, c], snp=partner(b)),
        )

    def code(b, g, c):
        block = pack(part[block_at(g, c)], GROUPS[g][1])
        mean = jnp.sum(block, axis=0, keepdims=True) * F32(1.0 / ex_rows(g))
        block = block - mean
        top = jnp.maximum(jnp.max(jnp.abs(block), axis=0, keepdims=True), F32(1e-30))
        coded[b - 1, g, c, :ex_rows(g), :] = jnp.round(block * (F32(LEVELS) / top)).astype(jnp.int32).astype(jnp.int16)
        first = lax.broadcasted_iota(jnp.int32, (8, lanes), 0) == 0
        meta[b - 1, g, c] = jnp.where(first, top * F32(1.0 / LEVELS), mean)
        for cp in ex_copies(b, g, c):
            cp.start()

    def arrived(b, g, c):
        for cp in ex_copies(b, g, c):
            cp.wait()
        side = GROUPS[g][1]
        other = coded_rx[b - 1, g, c, :ex_rows(g), :].astype(jnp.int32).astype(F32) * meta_rx[b - 1, g, c, 0:1, :]
        other = unpack(other + meta_rx[b - 1, g, c, 1:2, :], side)
        if side is not None:
            low = lower_lanes(other.shape)
            other = jnp.where(low if side == 0 else jnp.logical_not(low), other, F32(0.0))
        return part[block_at(g, c)] + other

    def ag_copy(h, c):
        seg = at(c, bit, krow)
        return copy(scores.at[h, seg], scores.at[h, seg], ag_s.at[h, c], ag_r.at[h, c], snp=partner(0))

    for g in range(groups):
        for c in range(chunks):
            h, side = GROUPS[g]
            if side != 1:
                rs_copy(h, c).wait()
                seg = block_at(g, c)
                part[seg] = part[seg] + rs_rx[c * krow:(c + 1) * krow, h * lanes:(h + 1) * lanes]
            if bits > 1:
                code(1, g, c)
    with jax.named_scope("dose_t"):
        word_t = g_ref[...].T
        for c in range(chunks):
            for t in range(PLANES):
                off = c * crow + t * cwords
                dose_t[:, off:off + cwords] = ((word_t[:, c * cwords:(c + 1) * cwords] >> (2 * t)) & 3).astype(F32).astype(BF16)
    for b in range(2, bits):
        for g in range(groups):
            for c in range(chunks):
                part[block_at(g, c)] = arrived(b - 1, g, c)
                code(b, g, c)
    cs_rx[me] = cs_tx[...]
    with jax.named_scope("center"):
        each(devices - 1, cs_wait)
    tot = lax.fori_loop(1, devices, lambda j, acc: acc + cs_rx[j], cs_rx[0], unroll=devices <= 16)
    center = jnp.concatenate([tot[0:1, :], tot[1:2, :]], axis=1) / F32(samples)

    def finish_scores(g):
        h = GROUPS[g][0]
        for c in range(chunks):
            total = arrived(bits - 1, g, c) if bits > 1 else part[block_at(g, c)]
            scores[g, at(c, bit, krow), :] = (total - center[:, h * lanes:(h + 1) * lanes]).astype(BF16)
            ag_copy(g, c).start()

    def gather_scores(h):
        for c in range(chunks):
            ag_copy(h, c).wait()

    inv_root = F32(1.0) / jnp.sqrt(F32(samples))
    last = n_samp - 1
    relay = n_samp >= 4
    mirrored = samp >= n_samp // 2
    place = jnp.where(mirrored, last - samp, samp)
    slots = n_samp - 1

    def y_part(h, owner):
        blk = dose_t[pl.ds(pl.multiple_of(owner * own_rows, 16), own_rows), :]
        return jnp.dot(blk, scores[h], preferred_element_type=F32) * inv_root

    def owner_of(k):
        k = jnp.int32(k)
        inner = jnp.where(k == 0, 1, jnp.where(k == 1, last, k))
        v = lax.rem(place + jnp.where(place == 0, last - k, inner), n_samp)
        return jnp.where(mirrored, last - v, v)

    def y_rows(h):
        return own_rows if GROUPS[h][1] is None else own_rows // 2

    def y_seg(h):
        return pl.ds(0, y_rows(h))

    def y_copies(h, k):
        to, slot = owner_of(k), samp
        if relay:
            handed = jnp.logical_and(place == 0, k == 0)
            to = jnp.where(handed, jnp.where(mirrored, last - 1, 1), to)
            slot = jnp.where(handed, to, samp)
        return (
            copy(yq.at[h, k, y_seg(h)], yq_rx.at[h, slot, y_seg(h)], yq_s.at[h, k], yq_r.at[h, slot], samp=to),
            copy(ysc.at[h, k], ysc_rx.at[h, slot], ysc_s.at[h, k], ysc_r.at[h, slot], samp=to),
        )

    def y_wait(h, slot):
        copy(yq.at[h, 0, y_seg(h)], yq_rx.at[h, slot, y_seg(h)], yq_s.at[h, 0], yq_r.at[h, slot], samp=samp).wait_recv()
        copy(ysc.at[h, 0], ysc_rx.at[h, slot], ysc_s.at[h, 0], ysc_r.at[h, slot], samp=samp).wait_recv()

    def y_decode(h, slot):
        return yq_rx[h, slot, :y_rows(h), :].astype(jnp.int32).astype(F32) * ysc_rx[h, slot, 0:1, :]

    def y_send(h, k, block):
        top = jnp.maximum(jnp.max(jnp.abs(block), axis=0, keepdims=True), F32(1e-30))
        yq[h, k, :y_rows(h), :] = jnp.round(block * (F32(LEVELS) / top)).astype(jnp.int32).astype(jnp.int16)
        ysc[h, k] = jnp.broadcast_to(top * F32(1.0 / LEVELS), (8, lanes))
        for cp in y_copies(h, k):
            cp.start()

    def y_first(h):
        each(slots - 1 if relay else slots, lambda k: y_send(h, k, pack(y_part(h, owner_of(k)), GROUPS[h][1])))

    def y_rest(h):
        if relay:
            @pl.when(place != 1)
            def _():
                y_send(h, slots - 1, pack(y_part(h, owner_of(slots - 1)), GROUPS[h][1]))

            @pl.when(place == 1)
            def _():
                y_tmp[h, :y_rows(h), :] = pack(y_part(h, owner_of(slots - 1)), GROUPS[h][1])
        y_own[h] = y_part(h, samp)

    def y_merge(h):
        if relay:
            @pl.when(place == 1)
            def _():
                y_wait(h, samp)
                y_send(h, slots - 1, y_tmp[h, :y_rows(h), :] + y_decode(h, samp))

    def y_finish(h):
        def add(i):
            src = lax.rem(samp + 1 + i, n_samp)
            if relay:
                @pl.when(jnp.logical_or(place != 0, src != last - samp))
                def _():
                    y_wait(h, src)
                    y_own[h] = y_own[h] + unpack(y_decode(h, src), GROUPS[h][1])
            else:
                y_wait(h, src)
                y_own[h] = y_own[h] + unpack(y_decode(h, src), GROUPS[h][1])

        each(slots, add)

    snp_total = F32(dose_t.shape[0] * n_snp)

    def gram_of(a, b):
        return lax.dot_general(a, b, (((0,), (0,)), ((), ())), precision=HIGH, preferred_element_type=F32) / snp_total

    def all_sum(work, rx, out, s1, r1, s2, r2):
        size, owners = pieces(work.shape[0], devices)

        def peer_of(i):
            return lax.rem(me + 1 + i, devices)

        def piece(i):
            return pl.ds(pl.multiple_of(i * size, 8), size)

        def where_owner(i, body):
            if owners == devices:
                body()
            else:
                pl.when(i < owners)(body)

        def one(i):
            p = peer_of(i)
            return p, copy(work.at[piece(p)], rx.at[me], s1.at[p], r1.at[me], samp=p // n_snp, snp=lax.rem(p, n_snp))

        def two(i):
            p = peer_of(i)
            return p, copy(out.at[piece(me)], out.at[piece(me)], s2.at[p], r2.at[me], samp=p // n_snp, snp=lax.rem(p, n_snp))

        def start():
            def go(i):
                p, cp = one(i)
                where_owner(p, lambda: cp.start())
            each(devices - 1, go)

        def middle():
            def owned():
                rx[me] = work[piece(me), :]

                def got(i):
                    p = peer_of(i)
                    copy(work.at[piece(0)], rx.at[p], s1.at[p], r1.at[p], samp=samp).wait_recv()
                each(devices - 1, got)
                total = lax.fori_loop(1, devices, lambda j, acc: acc + rx[j], rx[0], unroll=devices <= 16)
                out[piece(me), :] = total
                each(devices - 1, lambda i: two(i)[1].start())
            where_owner(me, owned)

        def finish():
            def got(i):
                p = peer_of(i)
                where_owner(p, lambda: copy(out.at[piece(0)], out.at[piece(p)], s2.at[p], r2.at[p], samp=samp).wait_recv())
            each(devices - 1, got)

        def drain():
            def sent(i):
                p, cp = one(i)
                where_owner(p, lambda: cp.wait_send())
            each(devices - 1, sent)
            where_owner(me, lambda: each(devices - 1, lambda i: two(i)[1].wait_send()))

        return start, middle, finish, drain

    a_start, a_middle, a_finish, a_drain = all_sum(ga_w, ga_rx, ga_out, ga_s, ga_r, ha_s, ha_r)
    b_start, b_middle, b_finish, b_drain = all_sum(gb_w, gb_rx, gb_out, gb_s, gb_r, hb_s, hb_r)

    for g in range(groups):
        with jax.named_scope("scores"):
            if g == 0:
                finish_scores(g)
            if g:
                y_merge(g - 1)
            gather_scores(g)
        with jax.named_scope("y_sent"):
            y_first(g)
            y_rest(g)
            if g + 1 < groups:
                finish_scores(g + 1)
    with jax.named_scope("y_kept"):
        y_finish(0)
        y_finish(1)
        y0 = jnp.where(lower_lanes((own_rows, lanes)), y_own[0], y_own[1])
        y_ref[:, :lanes] = y0
        ga_w[...] = gram_of(y0, y0)
        a_start()
    with jax.named_scope("y_kept_last"):
        y_merge(2)
        a_middle()
        y_finish(2)
        y1 = y_own[2]
        y_ref[:, lanes:] = y1
    gb_w[:lanes, :] = gram_of(y_ref[:, :lanes], y1)
    gb_w[lanes:, :] = gram_of(y1, y1)
    b_start()
    b_middle()
    a_finish()
    d_row, d_col = diagonal(ga_out[...])
    d_ref[...] = jnp.broadcast_to(d_row, d_ref.shape)
    up_ref[...], inv_ref[...] = eliminate(scaled(ga_out[...], d_col, d_row))
    b_finish()
    gb_ref[...] = gb_out[...]
    with jax.named_scope("drain"):
        each(devices - 1, lambda i: cs_copy(i).wait_send())
        for g in range(groups):
            def sent(k):
                for cp in y_copies(g, k):
                    cp.wait_send()
            each(slots, sent)
        a_drain()
        b_drain()


def per_device(n_snp, n_samp, genotypes, basis_cols):
    words, snps = genotypes.shape
    width = basis_cols.shape[1]
    rows = PLANES * words
    lanes = width // 2
    chunks = max(1, words // 128)
    own = snps // n_samp
    bits = log2(n_snp)
    devices = n_snp * n_samp
    krow = rows // chunks // 2
    steps = max(1, bits - 1)
    groups = len(GROUPS)
    vmem = pl.BlockSpec(memory_space=pltpu.VMEM)
    hbm = pl.BlockSpec(memory_space=pltpu.HBM)
    dma = pltpu.SemaphoreType.DMA
    size_a, size_b = pieces(lanes, devices)[0], pieces(width, devices)[0]
    y, gb, up, inv, diag = pl.pallas_call(
        functools.partial(main_kernel, n_snp, n_samp),
        out_shape=(
            pltpu.VMEM((own, width), F32),
            pltpu.VMEM((width, lanes), F32),
            pltpu.VMEM((lanes, lanes), F32),
            pltpu.VMEM((lanes, lanes), F32),
            pltpu.VMEM((8, lanes), F32),
        ),
        in_specs=[hbm, hbm],
        out_specs=(vmem,) * 5,
        scratch_shapes=[
            pltpu.VMEM((words, snps), jnp.int32),
            pltpu.VMEM((snps, width), BF16),
            pltpu.VMEM((rows, width), F32),
            pltpu.VMEM((rows // 2, width), F32),
            pltpu.VMEM((steps, groups, chunks, krow, lanes), jnp.int16),
            pltpu.VMEM((steps, groups, chunks, krow, lanes), jnp.int16),
            pltpu.VMEM((steps, groups, chunks, 8, lanes), F32),
            pltpu.VMEM((steps, groups, chunks, 8, lanes), F32),
            pltpu.VMEM((groups, rows, lanes), BF16),
            pltpu.VMEM((snps, rows), BF16),
            pltpu.VMEM((8, lanes), F32),
            pltpu.VMEM((devices, 8, lanes), F32),
            pltpu.VMEM((groups, own, lanes), F32),
            pltpu.VMEM((groups, own, lanes), F32),
            pltpu.VMEM((groups, n_samp, own, lanes), jnp.int16),
            pltpu.VMEM((groups, n_samp, 8, lanes), F32),
            pltpu.VMEM((groups, n_samp, own, lanes), jnp.int16),
            pltpu.VMEM((groups, n_samp, 8, lanes), F32),
            pltpu.VMEM((lanes, lanes), F32),
            pltpu.VMEM((devices, size_a, lanes), F32),
            pltpu.VMEM((lanes, lanes), F32),
            pltpu.VMEM((width, lanes), F32),
            pltpu.VMEM((devices, size_b, lanes), F32),
            pltpu.VMEM((width, lanes), F32),
            dma((chunks + 1,)),
            dma((2, chunks)), dma((2, chunks)),
            dma((steps, groups, chunks)), dma((steps, groups, chunks)), dma((steps, groups, chunks)), dma((steps, groups, chunks)),
            dma((groups, chunks)), dma((groups, chunks)),
            dma((devices,)), dma((devices,)),
            dma((groups, n_samp)), dma((groups, n_samp)), dma((groups, n_samp)), dma((groups, n_samp)),
            dma((devices,)), dma((devices,)), dma((devices,)), dma((devices,)),
            dma((devices,)), dma((devices,)), dma((devices,)), dma((devices,)),
        ],
        compiler_params=pltpu.CompilerParams(
            collective_id=0, has_side_effects=True, vmem_limit_bytes=60 * 1024 * 1024
        ),
    )(genotypes, basis_cols)
    y, r_factor, q_next = pl.pallas_call(
        factor_kernel,
        out_shape=(
            jax.ShapeDtypeStruct((own, width), F32),
            jax.ShapeDtypeStruct((width, width), F32),
            jax.ShapeDtypeStruct((own, width), F32),
        ),
        in_specs=[vmem] * 5,
        out_specs=(hbm,) * 3,
        scratch_shapes=[
            pltpu.VMEM((width, width), F32),
            pltpu.VMEM((2, own, lanes), F32),
            dma((6,)),
        ],
        compiler_params=pltpu.CompilerParams(vmem_limit_bytes=16 * 1024 * 1024),
    )(gb, up, inv, diag, y)
    layout = (1, 1, own, width)
    return (y.reshape(layout), r_factor, q_next.reshape(layout))


def solution(mesh):
    return jax.shard_map(
        functools.partial(per_device, mesh.shape["snp"], mesh.shape["samp"]),
        mesh=mesh,
        in_specs=(P(("grp", "samp"), "snp"), P(("grp", "snp"), None)),
        out_specs=(
            P(("grp", "snp"), "samp", None, None),
            P("grp", None),
            P(("grp", "snp"), "samp", None, None),
        ),
        check_vma=False,
    )
```
